768 devices in a mesh: silo: 64 (over y, z_hi, core), fsdp: 12 (over x, z_lo).
Axes of the slice: x: 4, y: 8, z: 12 (z_hi: 4, z_lo: 3; z = z_hi * 3 + z_lo), core: 2. Of those that a mesh axis runs over, the one named last changes fastest.
Arguments:
- activations: bfloat16 [64, 3072, 2304], P('silo', 'fsdp'), may hold values from -6 to 6
- key_cot: bfloat16 [64, 3072, 512], P('silo', 'fsdp'), may hold values from -0.29882812 to 0.29882812
- key_weight: bfloat16 [64, 2304, 512], P('silo', 'fsdp'), may hold values from -0.125 to 0.125
- weight_first: float32 [64, 2304, 512], P('silo', 'fsdp'), may hold values from -2 to 2
- weight_second: float32 [64, 2304, 512], P('silo', 'fsdp'), may hold values from 1 to 16
- norm_gain: float32 [64, 2304], P('silo', 'fsdp'), may hold values from 0.5 to 1.5
- gain_first: float32 [64, 2304], P('silo', 'fsdp'), may hold values from -2 to 2
- gain_second: float32 [64, 2304], P('silo', 'fsdp'), may hold values from 0.5 to 4
- pseudo_grad: bfloat16 [64, 4718592], P('silo', 'fsdp'), may hold values from -6 to 6
- outer_params: float32 [4718592], P('fsdp'), may hold values from -6 to 6
- outer_mom: float32 [4718592], P('fsdp'), may hold values from -3 to 3
Outputs:
- keys: bfloat16 [64, 3072, 512], P('silo', 'fsdp')
- new_weight: bfloat16 [64, 2304, 512], P('silo', 'fsdp')
- new_weight_first: float32 [64, 2304, 512], P('silo', 'fsdp')
- new_weight_second: float32 [64, 2304, 512], P('silo', 'fsdp')
- new_gain: float32 [64, 2304], P('silo', 'fsdp')
- new_gain_first: float32 [64, 2304], P('silo', 'fsdp')
- new_gain_second: float32 [64, 2304], P('silo', 'fsdp')
- new_outer_params: float32 [4718592], P('fsdp')
- new_outer_mom: float32 [4718592], P('fsdp')
The draws below stay inside these ranges and needn't reach their ends.
All inputs are finite; a program needn't handle non-finite values.
Results may differ from the reference program's by a relative error of at most 0.0095.
Values may be sent and summed in bfloat16 or wider, within the bound.
A program may use at most 64 MiB of HBM per device.

```python
import math
import jax
import jax.numpy as jnp
from jax import lax

FEAT = 2304
KVW = 512
TOK_DEV = 256
SILOS = 64
TOK_SILO = 3072
FRAG = 4718592
N_SILO = 64
N_FSDP = 12


def shard_levels(own_key, dims, shards, low, top_value):
    loudness, own = 1.0, jax.random.fold_in(own_key, 6)
    for dim, shards_of in shards:
        steps = jnp.exp(jax.random.uniform(jax.random.fold_in(own, dim), (shards_of,), jnp.float32, low / len(shards), top_value / len(shards)))
        loudness = loudness * jnp.repeat(steps, dims[dim] // shards_of).reshape([-1 if axis == dim else 1 for axis in range(len(dims))])
    return loudness


def bell_draw(key, shape, deviation, reach, split=(), kind=jnp.bfloat16):
    entries = jax.random.normal(key, shape, jnp.float32) * deviation
    if len(split) > 0:
        entries = shard_levels(key, shape, split, -0.22, 0.18) * entries
    return jnp.clip(entries, min=-reach, max=reach).astype(kind)


def setup_inputs(seed: int = 0) -> dict:
    streams_of = jax.random.split(jax.random.key(seed), 12)
    return {
        "activations": bell_draw(streams_of[0], (SILOS, TOK_SILO, FEAT), 1.0, 6.0, ((0, 64), (1, 12))),
        "key_cot": bell_draw(streams_of[1], (SILOS, TOK_SILO, KVW), 0.05, 0.29882812, ((0, 64), (1, 12))),
        "key_weight": bell_draw(streams_of[2], (SILOS, FEAT, KVW), FEAT ** -0.5, 0.125, ((0, 64), (1, 12))),
        "weight_first": bell_draw(streams_of[3], (SILOS, FEAT, KVW), 0.3, 2.0, ((0, 64), (1, 12)), jnp.float32),
        "weight_second": jnp.clip(jnp.exp(math.log(16.0) - 2.7725887 * jax.random.uniform(streams_of[4], (SILOS, FEAT, KVW), jnp.float32) ** shard_levels(streams_of[4], (SILOS, FEAT, KVW), ((0, 64), (1, 12)), -0.2, 0.2)), 1.0, 16.0),
        "norm_gain": jnp.clip(1.0 + 0.1 * jax.random.normal(streams_of[5], (SILOS, FEAT), jnp.float32), 0.5, 1.5),
        "gain_first": bell_draw(streams_of[6], (SILOS, FEAT), 0.3, 2.0, ((0, 64), (1, 12)), jnp.float32),
        "gain_second": jnp.clip(jnp.exp(math.log(4.0) - 2.0794415 * jax.random.uniform(streams_of[7], (SILOS, FEAT), jnp.float32) ** shard_levels(streams_of[7], (SILOS, FEAT), ((0, 64), (1, 12)), -0.2, 0.2)), 0.5, 4.0),
        "pseudo_grad": bell_draw(streams_of[8], (SILOS, FRAG), 1.0, 6.0, ((0, 64), (1, 12))),
        "outer_params": bell_draw(streams_of[9], (FRAG,), 1.0, 6.0, ((0, 12),), jnp.float32),
        "outer_mom": bell_draw(streams_of[10], (FRAG,), 0.5, 3.0, ((0, 12),), jnp.float32),
    }


norm_eps = 1e-05
beta_one = 0.9
beta_two = 0.95
corr_one = 1.0 - math.exp(200.0 * math.log(0.9))
corr_two = 1.0 - math.exp(200.0 * math.log(0.95))
learn_rate = 0.001
adam_eps = 1e-08
weight_decay = 0.1
outer_beta = 0.9
outer_rate = 0.7

def adam_step(params, gradient, first_moment, second_moment):
    first_new = beta_one * first_moment + (1.0 - beta_one) * gradient
    second_new = beta_two * second_moment + (1.0 - beta_two) * gradient * gradient
    update = first_new / corr_one / (jnp.sqrt(second_new / corr_two) + adam_eps) + weight_decay * params
    return (params - learn_rate * update, first_new, second_new)

def silo_step(silo_items):
    inputs, cotangent, weight, first_moment, second_moment, gain, gain_first, gain_second = silo_items
    wide_inputs = inputs.astype(jnp.float32)
    inv_rms = lax.rsqrt(lax.optimization_barrier(jnp.mean(wide_inputs * wide_inputs, axis=1, keepdims=True)) + norm_eps)
    gain_used = lax.optimization_barrier(gain.astype(jnp.bfloat16)).astype(jnp.float32)
    normed = (wide_inputs * inv_rms * gain_used[None, :]).astype(jnp.bfloat16)
    key_out = jnp.dot(normed, weight, preferred_element_type=jnp.float32).astype(jnp.bfloat16)
    back_grad = lax.dot_general(cotangent, weight, (((1,), (1,)), ((), ())), preferred_element_type=jnp.float32)
    gain_grad = lax.optimization_barrier(jnp.sum(back_grad * wide_inputs * inv_rms, axis=0))
    group_normed = normed.reshape(N_FSDP, TOK_DEV, FEAT).astype(jnp.float32)
    group_cot = cotangent.reshape(N_FSDP, TOK_DEV, KVW).astype(jnp.float32)
    partial_value = jnp.einsum('ntf,ntk->nfk', group_normed, group_cot)
    rounded = lax.optimization_barrier(partial_value.astype(jnp.bfloat16)).astype(jnp.float32)
    weight_grad = lax.optimization_barrier(jnp.sum(rounded, axis=0))
    new_weight, new_first, new_second = adam_step(weight.astype(jnp.float32), weight_grad, first_moment, second_moment)
    new_gain, new_gain_first, new_gain_second = adam_step(gain, gain_grad, gain_first, gain_second)
    return (key_out, new_weight.astype(jnp.bfloat16), new_first, new_second, new_gain, new_gain_first, new_gain_second)

def reference(activations, key_cot, key_weight, weight_first, weight_second, norm_gain, gain_first, gain_second, pseudo_grad, outer_params, outer_mom):
    results = lax.map(silo_step, (activations, key_cot, key_weight, weight_first, weight_second, norm_gain, gain_first, gain_second))
    silo_total = lax.optimization_barrier(jnp.sum(pseudo_grad, axis=0, dtype=jnp.float32))
    outer_delta = silo_total / N_SILO
    new_mom = outer_beta * outer_mom + outer_delta
    new_params = outer_params - outer_rate * (outer_delta + outer_beta * new_mom)
    return (results[0], results[1], results[2], results[3], results[4], results[5], results[6], new_params, new_mom)
```

```python
import math

import jax
import jax.numpy as jnp
from jax import lax
from jax.experimental import pallas as pl
from jax.experimental.pallas import tpu as pltpu
from jax.sharding import PartitionSpec as P

norm_eps = 1e-05
beta_one = 0.9
beta_two = 0.95
corr_one = 1.0 - math.exp(200.0 * math.log(0.9))
corr_two = 1.0 - math.exp(200.0 * math.log(0.95))
learn_rate = 0.001
adam_eps = 1e-08
weight_decay = 0.1
outer_beta = 0.9
outer_rate = 0.7

MESH = pl.DeviceIdType.MESH
NX, NZL = 4, 3
NY, NZH, NC = 8, 4, 2
NF, NS = NX * NZL, NY * NZH * NC
FEAT, KVW, TOK = 2304, 512, 256
ROWS = FEAT // NF
HALF = ROWS // 2
FROWS = 3072
CROWS = FROWS // NC
YROWS = CROWS // NY
ZROWS = YROWS // NZH
F32, BF16 = jnp.float32, jnp.bfloat16


class Slots:
    def __init__(self):
        self.index = {}

    def __call__(self, *name):
        return self.index.setdefault(name, len(self.index))


def kernel(slots, act_hbm, cot_hbm, w_hbm, gain_ref, pg_ref, keys_ref, gsum_ref, delta_ref,
           act, cot, w, xhat, wfull, gbuf, rx1, rx2, zsend, zrecv,
           psend, precv, hsum, yrecv, hz, zhrecv, dbuf, lsem, ssem, rsem):
    s, f = lax.axis_index("silo"), lax.axis_index("fsdp")
    core = lax.rem(s, NC)
    zh = lax.rem(s // NC, NZH)
    y = s // (NC * NZH)
    x, zl = f // NZL, lax.rem(f, NZL)

    def silo_at(yy, zz, cc):
        return (yy * NZH + zz) * NC + cc

    def fsdp_at(xx, zz):
        return xx * NZL + zz

    def to_y(d):
        return {"silo": silo_at(lax.rem(y + d, NY), zh, core), "fsdp": f}

    def to_zh(d):
        return {"silo": silo_at(y, lax.rem(zh + d, NZH), core), "fsdp": f}

    def to_zl(d):
        return {"silo": s, "fsdp": fsdp_at(x, lax.rem(zl + d, NZL))}

    def to_x(d):
        return {"silo": s, "fsdp": fsdp_at(lax.rem(x + d + NX, NX), zl)}

    partner = {"silo": silo_at(y, zh, 1 - core), "fsdp": f}
    peers = ([partner] + [to_y(d) for d in range(1, NY)] + [to_zh(d) for d in range(1, NZH)]
             + [to_zl(d) for d in range(1, NZL)] + [to_x(1), to_x(-1)])
    pending = []

    def remote(src, dst, device, *name):
        k = slots(*name)
        return pltpu.make_async_remote_copy(
            src_ref=src, dst_ref=dst, send_sem=ssem.at[k], recv_sem=rsem.at[k],
            device_id=device, device_id_type=MESH)

    def send(src, dst, device, *name):
        copy = remote(src, dst, device, *name)
        copy.start()
        pending.append(copy)

    def arrived(ref, *name):
        remote(ref, ref, partner, *name).wait_recv()

    barrier = pltpu.get_barrier_semaphore()
    for peer in peers:
        pl.semaphore_signal(barrier, inc=1, device_id=peer, device_id_type=MESH)

    loads = [pltpu.make_async_copy(a, b, lsem.at[i])
             for i, (a, b) in enumerate(((w_hbm, w), (cot_hbm, cot), (act_hbm, act)))]
    for load in loads:
        load.start()

    def rows(start, size):
        return pl.ds(pl.multiple_of(start, 16), size)

    psend[...] = pg_ref[rows((1 - core) * CROWS, CROWS), :].astype(BF16)

    loads[0].wait()
    diag = lax.broadcasted_iota(jnp.int32, (ROWS, ROWS), 0) == lax.broadcasted_iota(jnp.int32, (ROWS, ROWS), 1)
    gain_row = gain_ref[...].astype(BF16).astype(F32)
    gain_col = jnp.sum(jnp.where(diag, gain_row, 0.0), axis=1, keepdims=True)
    wfull[rows(f * ROWS, ROWS), :] = (w[0].astype(F32) * gain_col).astype(BF16)

    def wrows(xx, zz):
        return wfull.at[rows(fsdp_at(xx, zz) * ROWS, ROWS), :]

    def whalf(xx, zz, h):
        return wfull.at[rows(fsdp_at(xx, zz) * ROWS + h * HALF, HALF), :]

    pl.semaphore_wait(barrier, len(peers))

    send(psend, precv, partner, "pair")
    own_w = wrows(x, zl)
    send(own_w, own_w, to_x(1), "wx", 0, 1)
    send(own_w, own_w, to_x(-1), "wx", 0, -1)
    for d in range(1, NZL):
        send(own_w, own_w, to_zl(d), "wz", d)

    loads[2].wait()

    def norm_step(i, carry):
        at = rows(i * 16, 16)
        wide = act[0, at, :].astype(F32)
        inv = lax.rsqrt(jnp.sum(wide * wide, axis=1, keepdims=True) * (1.0 / FEAT) + norm_eps)
        xhat[at, :] = (wide * inv).astype(BF16)
        return carry

    lax.fori_loop(0, TOK // 16, norm_step, 0)

    arrived(precv, "pair")
    hsum[...] = (pg_ref[rows(core * CROWS, CROWS), :] + precv[...].astype(F32)).astype(BF16)
    for d in range(1, NY):
        send(hsum.at[rows(lax.rem(y + d, NY) * YROWS, YROWS), :], yrecv.at[d - 1], to_y(d), "yr", d)

    loads[1].wait()
    step = 2 * ROWS
    for j in range(FEAT // step):
        gbuf[j * step:(j + 1) * step, :] = lax.dot_general(
            xhat[:, j * step:(j + 1) * step], cot[0], (((0,), (0,)), ((), ())),
            preferred_element_type=F32).astype(BF16)

    def grows(xx, zz):
        return gbuf.at[rows(fsdp_at(xx, zz) * ROWS, ROWS), :]

    def ghalf(xx, zz, h):
        return gbuf.at[rows(fsdp_at(xx, zz) * ROWS + h * HALF, HALF), :]

    right, left, far = lax.rem(x + 1, NX), lax.rem(x + 3, NX), lax.rem(x + 2, NX)
    for zz in range(NZL):
        send(ghalf(far, zz, 0), rx1.at[0, zz], to_x(1), "g1", zz, 1)
        send(ghalf(far, zz, 1), rx1.at[1, zz], to_x(-1), "g1", zz, -1)

    def pass_on(j):
        zz = lax.rem(zl - j + NZL, NZL)
        arrived(wrows(left, zz), "wx", j, 1)
        send(whalf(left, zz, 0), whalf(left, zz, 0), to_x(1), "wf", j, 1)
        arrived(wrows(right, zz), "wx", j, -1)
        send(whalf(right, zz, 1), whalf(right, zz, 1), to_x(-1), "wf", j, -1)

    pass_on(0)

    for zz in range(NZL):
        arrived(rx1.at[0, zz], "g1", zz, 1)
        up = ghalf(right, zz, 0)
        up[...] = (up[...].astype(F32) + rx1[0, zz].astype(F32)).astype(BF16)
        send(grows(right, zz), rx2.at[0, zz], to_x(1), "g2", zz, 1)
        arrived(rx1.at[1, zz], "g1", zz, -1)
        down = ghalf(left, zz, 1)
        down[...] = (down[...].astype(F32) + rx1[1, zz].astype(F32)).astype(BF16)
        send(grows(left, zz), rx2.at[1, zz], to_x(-1), "g2", zz, -1)

    for d in range(1, NZL):
        zz = lax.rem(zl - d + NZL, NZL)
        arrived(wrows(x, zz), "wz", d)
        send(wrows(x, zz), wrows(x, zz), to_x(1), "wx", d, 1)
        send(wrows(x, zz), wrows(x, zz), to_x(-1), "wx", d, -1)

    for d in range(1, NY):
        arrived(yrecv.at[d - 1], "yr", d)
    total = hsum[rows(y * YROWS, YROWS), :].astype(F32)
    for d in range(1, NY):
        total = total + yrecv[d - 1].astype(F32)
    hz[...] = total.astype(BF16)
    for d in range(1, NZH):
        send(hz.at[rows(lax.rem(zh + d, NZH) * ZROWS, ZROWS), :], zhrecv.at[d - 1], to_zh(d), "zr", d)
    for d in range(1, NZH):
        arrived(zhrecv.at[d - 1], "zr", d)
    part = hz[rows(zh * ZROWS, ZROWS), :].astype(F32)
    for d in range(1, NZH):
        part = part + zhrecv[d - 1].astype(F32)

    def piece(yy, zz, cc):
        return dbuf.at[rows(cc * CROWS + yy * YROWS + zz * ZROWS, ZROWS), :]

    def chunk(yy, cc):
        return dbuf.at[rows(cc * CROWS + yy * YROWS, YROWS), :]

    piece(y, zh, core)[...] = (part * (1.0 / NS)).astype(BF16)
    for d in range(1, NZH):
        send(piece(y, zh, core), piece(y, zh, core), to_zh(d), "zg", d)
    for d in range(1, NZH):
        arrived(piece(y, lax.rem(zh - d + NZH, NZH), core), "zg", d)
    for d in range(1, NY):
        send(chunk(y, core), chunk(y, core), to_y(d), "yg", d)
    send(chunk(y, core), chunk(y, core), partner, "cg", 0)

    for i in range(NZL):
        d = (i + 1) % NZL
        zz = lax.rem(zl + d, NZL)
        both = grows(x, zz)[...].astype(F32)
        if i == 0:
            for z2 in range(NZL):
                arrived(rx2.at[0, z2], "g2", z2, 1)
                arrived(rx2.at[1, z2], "g2", z2, -1)
        both = both + rx2[0, zz].astype(F32) + rx2[1, zz].astype(F32)
        if d:
            zsend[d - 1] = both.astype(BF16)
            send(zsend.at[d - 1], zrecv.at[d - 1], to_zl(d), "gz", d)
        else:
            gsum_ref[...] = both

    for d in range(1, NZL):
        pass_on(d)

    for d in range(1, NY):
        yy = lax.rem(y - d + NY, NY)
        arrived(chunk(yy, core), "yg", d)
        send(chunk(yy, core), chunk(yy, core), partner, "cg", d)

    for d in range(1, NZL):
        arrived(zrecv.at[d - 1], "gz", d)
    gsum_ref[...] += zrecv[0].astype(F32) + zrecv[1].astype(F32)

    for j in range(NZL):
        zz = lax.rem(zl - j + NZL, NZL)
        arrived(whalf(far, zz, 0), "wf", j, 1)
        arrived(whalf(far, zz, 1), "wf", j, -1)
    keys_ref[...] = jnp.dot(xhat[...], wfull[...], preferred_element_type=F32).astype(BF16)

    for d in range(NY):
        arrived(chunk(lax.rem(y - d + NY, NY), 1 - core), "cg", d)
    delta_ref[...] = dbuf[...]
    for copy in pending:
        copy.wait_send()


def exchange(activations, key_cot, key_weight, norm_gain, fragment):
    slots = Slots()
    count = 64

    def body(*refs):
        kernel(slots, *refs)
        assert len(slots.index) <= count

    any_spec = pl.BlockSpec(memory_space=pl.ANY)
    vmem = pl.BlockSpec(memory_space=pltpu.VMEM)
    return pl.pallas_call(
        body,
        out_shape=(
            jax.ShapeDtypeStruct((TOK, KVW), BF16),
            jax.ShapeDtypeStruct((ROWS, KVW), F32),
            jax.ShapeDtypeStruct((FROWS, 128), BF16),
        ),
        in_specs=[any_spec, any_spec, any_spec, vmem, vmem],
        out_specs=(vmem, vmem, vmem),
        scratch_shapes=[
            pltpu.VMEM((1, TOK, FEAT), BF16),
            pltpu.VMEM((1, TOK, KVW), BF16),
            pltpu.VMEM((1, ROWS, KVW), BF16),
            pltpu.VMEM((TOK, FEAT), BF16),
            pltpu.VMEM((FEAT, KVW), BF16),
            pltpu.VMEM((FEAT, KVW), BF16),
            pltpu.VMEM((2, NZL, HALF, KVW), BF16),
            pltpu.VMEM((2, NZL, ROWS, KVW), BF16),
            pltpu.VMEM((NZL - 1, ROWS, KVW), BF16),
            pltpu.VMEM((NZL - 1, ROWS, KVW), BF16),
            pltpu.VMEM((CROWS, 128), BF16),
            pltpu.VMEM((CROWS, 128), BF16),
            pltpu.VMEM((CROWS, 128), BF16),
            pltpu.VMEM((NY - 1, YROWS, 128), BF16),
            pltpu.VMEM((YROWS, 128), BF16),
            pltpu.VMEM((NZH - 1, ZROWS, 128), BF16),
            pltpu.VMEM((FROWS, 128), BF16),
            pltpu.SemaphoreType.DMA((3,)),
            pltpu.SemaphoreType.DMA((count,)),
            pltpu.SemaphoreType.DMA((count,)),
        ],
        compiler_params=pltpu.CompilerParams(
            collective_id=0, has_side_effects=True, vmem_limit_bytes=32 << 20
        ),
    )(activations, key_cot, key_weight, norm_gain, fragment)


def adam_step(params, gradient, first_moment, second_moment):
    first_new = beta_one * first_moment + (1.0 - beta_one) * gradient
    second_new = beta_two * second_moment + (1.0 - beta_two) * gradient * gradient
    update = (
        first_new / corr_one / (jnp.sqrt(second_new / corr_two) + adam_eps) + weight_decay * params
    )
    return (params - learn_rate * update, first_new, second_new)


def per_device(
    activations,
    key_cot,
    key_weight,
    weight_first,
    weight_second,
    norm_gain,
    gain_first,
    gain_second,
    pseudo_grad,
    outer_params,
    outer_mom,
):
    fragment = pseudo_grad.astype(F32).reshape(FROWS, 128)
    keys, gsum, delta = exchange(activations, key_cot, key_weight, norm_gain, fragment)

    gain_used = norm_gain[0].astype(BF16).astype(F32)
    wide_weight = key_weight[0].astype(F32)
    new_weight, new_first, new_second = adam_step(
        wide_weight, gsum * gain_used[:, None], weight_first[0], weight_second[0]
    )
    gain_grad = jnp.sum(gsum * wide_weight, axis=1)
    new_gain, new_gain_first, new_gain_second = adam_step(
        norm_gain[0], gain_grad, gain_first[0], gain_second[0]
    )
    wide_delta = delta.astype(F32)
    new_mom = outer_beta * outer_mom.reshape(FROWS, 128) + wide_delta
    new_params = outer_params.reshape(FROWS, 128) - outer_rate * (wide_delta + outer_beta * new_mom)
    return (
        keys[None],
        new_weight.astype(BF16)[None],
        new_first[None],
        new_second[None],
        new_gain[None],
        new_gain_first[None],
        new_gain_second[None],
        new_params.reshape(-1),
        new_mom.reshape(-1),
    )


def solution(mesh):
    return jax.shard_map(
        per_device,
        mesh=mesh,
        in_specs=(
            P("silo", "fsdp", None),
            P("silo", "fsdp", None),
            P("silo", "fsdp", None),
            P("silo", "fsdp", None),
            P("silo", "fsdp", None),
            P("silo", "fsdp"),
            P("silo", "fsdp"),
            P("silo", "fsdp"),
            P("silo", "fsdp"),
            P("fsdp"),
            P("fsdp"),
        ),
        out_specs=(
            P("silo", "fsdp", None),
            P("silo", "fsdp", None),
            P("silo", "fsdp", None),
            P("silo", "fsdp", None),
            P("silo", "fsdp"),
            P("silo", "fsdp"),
            P("silo", "fsdp"),
            P("fsdp"),
            P("fsdp"),
        ),
        check_vma=False,
    )
```

```python
import math

import jax
import jax.numpy as jnp
from jax import lax
from jax.experimental import pallas as pl
from jax.experimental.pallas import tpu as pltpu
from jax.sharding import PartitionSpec as P

norm_eps = 1e-05
beta_one = 0.9
beta_two = 0.95
corr_one = 1.0 - math.exp(200.0 * math.log(0.9))
corr_two = 1.0 - math.exp(200.0 * math.log(0.95))
learn_rate = 0.001
adam_eps = 1e-08
weight_decay = 0.1
outer_beta = 0.9
outer_rate = 0.7

MESH = pl.DeviceIdType.MESH
NX, NZL = 4, 3
NY, NZH, NC = 8, 4, 2
NF, NS = NX * NZL, NY * NZH * NC
FEAT, KVW, TOK = 2304, 512, 256
ROWS = FEAT // NF
XROWS = FEAT // NX
XHALF = XROWS // 2
THALF = TOK // 2
FROWS = 3072
CROWS = FROWS // NC
YROWS = CROWS // NY
ZROWS = YROWS // NZH
F32, BF16 = jnp.float32, jnp.bfloat16


class Slots:
    def __init__(self):
        self.index = {}

    def __call__(self, *name):
        return self.index.setdefault(name, len(self.index))


def kernel(slots, act_hbm, cot_hbm, w_hbm, gain_hbm, pg_hbm, keys_ref, wgrad_ref, ggrad_ref, delta_ref,
           act, w, gain, pg, xhat, xt, xin, relay, cot, wx, kpart, kin1, kin2, kown, zsend, zrecv,
           psend, precv, hsum, yrecv, hz, zhrecv, dbuf, lsem, ssem, rsem):
    s, f = lax.axis_index("silo"), lax.axis_index("fsdp")
    core = lax.rem(s, NC)
    zh = lax.rem(s // NC, NZH)
    y = s // (NC * NZH)
    x, zl = f // NZL, lax.rem(f, NZL)

    def silo_at(yy, zz, cc):
        return (yy * NZH + zz) * NC + cc

    def fsdp_at(xx, zz):
        return xx * NZL + zz

    def to_y(d):
        return {"silo": silo_at(lax.rem(y + d, NY), zh, core), "fsdp": f}

    def to_zh(d):
        return {"silo": silo_at(y, lax.rem(zh + d, NZH), core), "fsdp": f}

    def to_zl(d):
        return {"silo": s, "fsdp": fsdp_at(x, lax.rem(zl + d, NZL))}

    def to_x(d):
        return {"silo": s, "fsdp": fsdp_at(lax.rem(x + d + NX, NX), zl)}

    partner = {"silo": silo_at(y, zh, 1 - core), "fsdp": f}
    peers = ([to_y(d) for d in range(1, NY)] + [to_zh(d) for d in range(1, NZH)]
             + [to_zl(d) for d in range(1, NZL)] + [to_x(1), to_x(-1)] + [partner])
    pending = []

    def remote(src, dst, device, *name):
        k = slots(*name)
        return pltpu.make_async_remote_copy(
            src_ref=src, dst_ref=dst, send_sem=ssem.at[k], recv_sem=rsem.at[k],
            device_id=device, device_id_type=MESH)

    def send(src, dst, device, *name):
        copy = remote(src, dst, device, *name)
        copy.start()
        pending.append(copy)

    def arrived(ref, *name):
        remote(ref, ref, partner, *name).wait_recv()

    barrier = pltpu.get_barrier_semaphore()
    for peer in peers:
        pl.semaphore_signal(barrier, inc=1, device_id=peer, device_id_type=MESH)

    loads = [pltpu.make_async_copy(a, b, lsem.at[i]) for i, (a, b) in enumerate((
        (w_hbm.at[0], w), (gain_hbm, gain), (cot_hbm.at[0], cot.at[0]), (pg_hbm, pg), (act_hbm.at[0], act)))]
    for load in loads:
        load.start()

    def rows(start, size):
        return pl.ds(pl.multiple_of(start, 16), size)

    loads[0].wait()
    loads[1].wait()
    diag = lax.broadcasted_iota(jnp.int32, (ROWS, ROWS), 0) == lax.broadcasted_iota(jnp.int32, (ROWS, ROWS), 1)
    gain_row = gain[...].astype(BF16).astype(F32)
    gain_col = jnp.sum(jnp.where(diag, gain_row, 0.0), axis=1, keepdims=True)

    def wrows(zz):
        return wx.at[rows(zz * ROWS, ROWS), :]

    wrows(zl)[...] = (w[...].astype(F32) * gain_col).astype(BF16)

    def lanes(start):
        return pg[0, pl.ds(pl.multiple_of(start, 2048), 2048)].reshape(16, 128)

    loads[3].wait()

    def pack_step(i, carry):
        psend[rows(i * 16, 16), :] = lanes((1 - core) * (CROWS * 128) + i * 2048)
        return carry

    lax.fori_loop(0, CROWS // 16, pack_step, 0, unroll=4)
    loads[2].wait()

    pl.semaphore_wait(barrier, len(peers))

    send(psend, precv, partner, "pair")
    send(cot.at[0], cot.at[1], to_x(1), "c", 1)
    send(cot.at[0], cot.at[3], to_x(-1), "c", -1)
    for d in range(1, NZL):
        send(wrows(zl), wrows(zl), to_zl(d), "wz", d)

    loads[4].wait()

    def norm_step(i, carry):
        at = rows(i * 16, 16)
        wide = act[at, :].astype(F32)
        inv = lax.rsqrt(jnp.sum(wide * wide, axis=1, keepdims=True) * (1.0 / FEAT) + norm_eps)
        xhat[at, :] = (wide * inv).astype(BF16)
        return carry

    lax.fori_loop(0, TOK // 16, norm_step, 0)

    arrived(precv, "pair")

    def sum_step(i, carry):
        at = rows(i * 16, 16)
        own = lanes(core * (CROWS * 128) + i * 2048)
        hsum[at, :] = (own.astype(F32) + precv[at, :].astype(F32)).astype(BF16)
        return carry

    lax.fori_loop(0, CROWS // 16, sum_step, 0, unroll=4)
    for d in (4, 3, 5, 2, 6, 1, 7):
        send(hsum.at[rows(lax.rem(y + d, NY) * YROWS, YROWS), :], yrecv.at[d - 1], to_y(d), "yr", d)

    for j in range(FEAT // 256):
        xt[j * 256:(j + 1) * 256, :] = xhat[:, j * 256:(j + 1) * 256].T

    right, left, far = lax.rem(x + 1, NX), lax.rem(x + 3, NX), lax.rem(x + 2, NX)

    def block(xx):
        return xt.at[rows(xx * XROWS, XROWS), :]

    def half(xx, h):
        return xt.at[rows(xx * XROWS + h * XHALF, XHALF), :]

    send(half(far, 0), relay.at[0], to_x(1), "r", 1)
    send(half(far, 1), relay.at[1], to_x(-1), "r", -1)
    send(block(right), xin.at[0], to_x(1), "x", 1)
    send(block(left), xin.at[2], to_x(-1), "x", -1)
    arrived(relay.at[0], "r", 1)
    send(relay.at[0], xin.at[1, pl.ds(0, XHALF), :], to_x(1), "f", 1)
    arrived(relay.at[1], "r", -1)
    send(relay.at[1], xin.at[1, pl.ds(XHALF, XHALF), :], to_x(-1), "f", -1)
    arrived(cot.at[1], "c", 1)
    send(cot.at[1, pl.ds(0, THALF), :], cot.at[2, pl.ds(0, THALF), :], to_x(1), "d", 1)
    arrived(cot.at[3], "c", -1)
    send(cot.at[3, pl.ds(THALF, THALF), :], cot.at[2, pl.ds(THALF, THALF), :], to_x(-1), "d", -1)

    for d in range(1, NZL):
        arrived(wrows(lax.rem(zl - d + NZL, NZL)), "wz", d)

    def partial_keys(ref):
        return lax.dot_general(ref[...], wx[...], (((0,), (0,)), ((), ())), preferred_element_type=F32)

    kown[...] = partial_keys(block(x))
    arrived(xin.at[0], "x", 1)
    kpart[0] = partial_keys(xin.at[0]).astype(BF16)
    arrived(xin.at[2], "x", -1)
    kpart[2] = partial_keys(xin.at[2]).astype(BF16)

    for d in range(1, NY):
        arrived(yrecv.at[d - 1], "yr", d)
    total = hsum[rows(y * YROWS, YROWS), :].astype(F32)
    for d in range(1, NY):
        total = total + yrecv[d - 1].astype(F32)
    hz[...] = total.astype(BF16)
    for d in range(1, NZH):
        send(hz.at[rows(lax.rem(zh + d, NZH) * ZROWS, ZROWS), :], zhrecv.at[d - 1], to_zh(d), "zr", d)

    arrived(xin.at[1, pl.ds(0, XHALF), :], "f", 1)
    arrived(xin.at[1, pl.ds(XHALF, XHALF), :], "f", -1)
    kpart[1] = partial_keys(xin.at[1]).astype(BF16)
    send(kpart.at[1, pl.ds(0, THALF), :], kin1.at[0], to_x(1), "k1", 1)
    send(kpart.at[1, pl.ds(THALF, THALF), :], kin1.at[1], to_x(-1), "k1", -1)

    for d in range(1, NZH):
        arrived(zhrecv.at[d - 1], "zr", d)
    part = hz[rows(zh * ZROWS, ZROWS), :].astype(F32)
    for d in range(1, NZH):
        part = part + zhrecv[d - 1].astype(F32)

    def piece(yy, zz, cc):
        return dbuf.at[rows(cc * CROWS + yy * YROWS + zz * ZROWS, ZROWS), :]

    def chunk(yy, cc):
        return dbuf.at[rows(cc * CROWS + yy * YROWS, YROWS), :]

    piece(y, zh, core)[...] = (part * (1.0 / NS)).astype(BF16)
    for d in range(1, NZH):
        send(piece(y, zh, core), piece(y, zh, core), to_zh(d), "zg", d)

    arrived(cot.at[2, pl.ds(0, THALF), :], "d", 1)
    arrived(cot.at[2, pl.ds(THALF, THALF), :], "d", -1)

    def product(zz):
        at = rows(zz * ROWS, ROWS)
        out = jnp.dot(xt[rows(x * XROWS + zz * ROWS, ROWS), :], cot[0], preferred_element_type=F32)
        for d in range(1, NX):
            out = out + jnp.dot(xin[d - 1, at, :], cot[d], preferred_element_type=F32)
        return out

    for d in range(1, NZL):
        zsend[d - 1] = product(lax.rem(zl + d, NZL)).astype(BF16)
        send(zsend.at[d - 1], zrecv.at[d - 1], to_zl(d), "gz", d)

    for d in range(1, NZH):
        arrived(piece(y, lax.rem(zh - d + NZH, NZH), core), "zg", d)
    for d in (4, 3, 5, 2, 6, 1, 7):
        send(chunk(y, core), chunk(y, core), to_y(d), "yg", d)
    send(chunk(y, core), chunk(y, core), partner, "cg", 0)

    arrived(kin1.at[0], "k1", 1)
    kpart[2, :THALF] = (kpart[2, :THALF].astype(F32) + kin1[0].astype(F32)).astype(BF16)
    send(kpart.at[2], kin2.at[0], to_x(1), "k2", 1)
    arrived(kin1.at[1], "k1", -1)
    kpart[0, THALF:] = (kpart[0, THALF:].astype(F32) + kin1[1].astype(F32)).astype(BF16)
    send(kpart.at[0], kin2.at[1], to_x(-1), "k2", -1)

    wgrad_ref[...] = product(zl)

    for d in (1, 7, 2, 6, 3, 5, 4):
        yy = lax.rem(y - d + NY, NY)
        arrived(chunk(yy, core), "yg", d)
        send(chunk(yy, core), chunk(yy, core), partner, "cg", d)

    arrived(kin2.at[0], "k2", 1)
    arrived(kin2.at[1], "k2", -1)
    keys_ref[...] = (kown[...] + kin2[0].astype(F32) + kin2[1].astype(F32)).astype(BF16)

    for d in range(1, NZL):
        arrived(zrecv.at[d - 1], "gz", d)
    gsum = wgrad_ref[...] + zrecv[0].astype(F32) + zrecv[1].astype(F32)
    gain_grad = jnp.sum(gsum * w[...].astype(F32), axis=1, keepdims=True)
    wgrad_ref[...] = gsum * gain_col
    ggrad_ref[...] = jnp.sum(jnp.where(diag, gain_grad, 0.0), axis=0, keepdims=True)

    for d in range(NY):
        arrived(chunk(lax.rem(y - d + NY, NY), 1 - core), "cg", d)
    delta_ref[...] = dbuf[...]
    for copy in pending:
        copy.wait_send()


def exchange(activations, key_cot, key_weight, norm_gain, pseudo_grad):
    slots = Slots()
    count = 64

    def body(*refs):
        kernel(slots, *refs)
        assert len(slots.index) <= count

    hbm = pl.BlockSpec(memory_space=pltpu.HBM)
    vmem = pl.BlockSpec(memory_space=pltpu.VMEM)
    return pl.pallas_call(
        body,
        out_shape=(
            jax.ShapeDtypeStruct((TOK, KVW), BF16),
            jax.ShapeDtypeStruct((ROWS, KVW), F32),
            jax.ShapeDtypeStruct((1, ROWS), F32),
            jax.ShapeDtypeStruct((FROWS, 128), BF16),
        ),
        in_specs=[hbm] * 5,
        out_specs=(vmem,) * 4,
        scratch_shapes=[
            pltpu.VMEM((TOK, FEAT), BF16),
            pltpu.VMEM((ROWS, KVW), BF16),
            pltpu.VMEM((1, ROWS), F32),
            pltpu.VMEM((1, FROWS * 128), BF16),
            pltpu.VMEM((TOK, FEAT), BF16),
            pltpu.VMEM((FEAT, TOK), BF16),
            pltpu.VMEM((NX - 1, XROWS, TOK), BF16),
            pltpu.VMEM((2, XHALF, TOK), BF16),
            pltpu.VMEM((NX, TOK, KVW), BF16),
            pltpu.VMEM((XROWS, KVW), BF16),
            pltpu.VMEM((NX - 1, TOK, KVW), BF16),
            pltpu.VMEM((2, THALF, KVW), BF16),
            pltpu.VMEM((2, TOK, KVW), BF16),
            pltpu.VMEM((TOK, KVW), F32),
            pltpu.VMEM((NZL - 1, ROWS, KVW), BF16),
            pltpu.VMEM((NZL - 1, ROWS, KVW), BF16),
            pltpu.VMEM((CROWS, 128), BF16),
            pltpu.VMEM((CROWS, 128), BF16),
            pltpu.VMEM((CROWS, 128), BF16),
            pltpu.VMEM((NY - 1, YROWS, 128), BF16),
            pltpu.VMEM((YROWS, 128), BF16),
            pltpu.VMEM((NZH - 1, ZROWS, 128), BF16),
            pltpu.VMEM((FROWS, 128), BF16),
            pltpu.SemaphoreType.DMA((5,)),
            pltpu.SemaphoreType.DMA((count,)),
            pltpu.SemaphoreType.DMA((count,)),
        ],
        compiler_params=pltpu.CompilerParams(
            collective_id=0, has_side_effects=True, vmem_limit_bytes=32 << 20
        ),
    )(activations, key_cot, key_weight, norm_gain, pseudo_grad)


def adam_step(params, gradient, first_moment, second_moment):
    first_new = beta_one * first_moment + (1.0 - beta_one) * gradient
    second_new = beta_two * second_moment + (1.0 - beta_two) * gradient * gradient
    update = (
        first_new / corr_one / (jnp.sqrt(second_new / corr_two) + adam_eps) + weight_decay * params
    )
    return (params - learn_rate * update, first_new, second_new)


def per_device(
    activations,
    key_cot,
    key_weight,
    weight_first,
    weight_second,
    norm_gain,
    gain_first,
    gain_second,
    pseudo_grad,
    outer_params,
    outer_mom,
):
    keys, weight_grad, gain_grad, delta = exchange(
        activations, key_cot, key_weight, norm_gain, pseudo_grad
    )
    new_weight, new_first, new_second = adam_step(
        key_weight[0].astype(F32), weight_grad, weight_first[0], weight_second[0]
    )
    new_gain, new_gain_first, new_gain_second = adam_step(
        norm_gain, gain_grad, gain_first, gain_second
    )
    wide_delta = delta.astype(F32)
    new_mom = outer_beta * outer_mom.reshape(FROWS, 128) + wide_delta
    new_params = outer_params.reshape(FROWS, 128) - outer_rate * (wide_delta + outer_beta * new_mom)
    return (
        keys[None],
        new_weight.astype(BF16)[None],
        new_first[None],
        new_second[None],
        new_gain,
        new_gain_first,
        new_gain_second,
        new_params.reshape(-1),
        new_mom.reshape(-1),
    )


def solution(mesh):
    return jax.shard_map(
        per_device,
        mesh=mesh,
        in_specs=(
            P("silo", "fsdp", None),
            P("silo", "fsdp", None),
            P("silo", "fsdp", None),
            P("silo", "fsdp", None),
            P("silo", "fsdp", None),
            P("silo", "fsdp"),
            P("silo", "fsdp"),
            P("silo", "fsdp"),
            P("silo", "fsdp"),
            P("fsdp"),
            P("fsdp"),
        ),
        out_specs=(
            P("silo", "fsdp", None),
            P("silo", "fsdp", None),
            P("silo", "fsdp", None),
            P("silo", "fsdp", None),
            P("silo", "fsdp"),
            P("silo", "fsdp"),
            P("silo", "fsdp"),
            P("fsdp"),
            P("fsdp"),
        ),
        check_vma=False,
    )
```

```python
import math

import jax
import jax.numpy as jnp
from jax import lax
from jax.experimental import pallas as pl
from jax.experimental.pallas import tpu as pltpu
from jax.sharding import PartitionSpec as P

norm_eps = 1e-05
beta_one = 0.9
beta_two = 0.95
corr_one = 1.0 - math.exp(200.0 * math.log(0.9))
corr_two = 1.0 - math.exp(200.0 * math.log(0.95))
learn_rate = 0.001
adam_eps = 1e-08
weight_decay = 0.1
outer_beta = 0.9
outer_rate = 0.7

MESH = pl.DeviceIdType.MESH
NX, NZL = 4, 3
NY, NZH, NC = 8, 4, 2
NF, NS = NX * NZL, NY * NZH * NC
FEAT, KVW, TOK = 2304, 512, 256
ROWS = FEAT // NF
XROWS = FEAT // NX
XHALF = XROWS // 2
THALF = TOK // 2
FROWS = 3072
CROWS = FROWS // NC
YROWS = CROWS // NY
YHALF = YROWS // 2
F32, BF16 = jnp.float32, jnp.bfloat16


class Slots:
    def __init__(self):
        self.index = {}

    def __call__(self, *name):
        return self.index.setdefault(name, len(self.index))


def kernel(slots, act_hbm, cot_hbm, w_hbm, gain_hbm, pg_hbm, keys_ref, wgrad_ref, ggrad_ref, delta_ref,
           act, w, gain, pg, xhat, xt, xin, relay, cot, wx, kpart, kin1, kin2, kown, zsend, zrecv,
           psend, precv, hsum, ya, yb, yc, yd, zall, dbuf, lsem, ssem, rsem):
    s, f = lax.axis_index("silo"), lax.axis_index("fsdp")
    core = lax.rem(s, NC)
    zh = lax.rem(s // NC, NZH)
    y = s // (NC * NZH)
    x, zl = f // NZL, lax.rem(f, NZL)

    def silo_at(yy, zz, cc):
        return (yy * NZH + zz) * NC + cc

    def fsdp_at(xx, zz):
        return xx * NZL + zz

    def to_y(d):
        return {"silo": silo_at(lax.rem(y + d, NY), zh, core), "fsdp": f}

    def to_zh(d):
        return {"silo": silo_at(y, lax.rem(zh + d, NZH), core), "fsdp": f}

    def to_zl(d):
        return {"silo": s, "fsdp": fsdp_at(x, lax.rem(zl + d, NZL))}

    def to_x(d):
        return {"silo": s, "fsdp": fsdp_at(lax.rem(x + d + NX, NX), zl)}

    partner = {"silo": silo_at(y, zh, 1 - core), "fsdp": f}
    peers = ([to_y(d) for d in (1, 2, 6, 7)] + [to_zh(d) for d in range(1, NZH)]
             + [to_zl(d) for d in range(1, NZL)] + [to_x(1), to_x(-1)] + [partner])
    pending = []

    def remote(src, dst, device, *name):
        k = slots(*name)
        return pltpu.make_async_remote_copy(
            src_ref=src, dst_ref=dst, send_sem=ssem.at[k], recv_sem=rsem.at[k],
            device_id=device, device_id_type=MESH)

    def send(src, dst, device, *name):
        copy = remote(src, dst, device, *name)
        copy.start()
        pending.append(copy)

    def arrived(ref, *name):
        remote(ref, ref, partner, *name).wait_recv()

    barrier = pltpu.get_barrier_semaphore()
    for peer in peers:
        pl.semaphore_signal(barrier, inc=1, device_id=peer, device_id_type=MESH)

    loads = [pltpu.make_async_copy(a, b, lsem.at[i]) for i, (a, b) in enumerate((
        (pg_hbm, pg), (cot_hbm.at[0], cot.at[0]), (w_hbm.at[0], w), (gain_hbm, gain), (act_hbm.at[0], act)))]
    for load in loads:
        load.start()

    def rows(start, size):
        return pl.ds(pl.multiple_of(start, 16), size)

    def lanes(start):
        return pg[0, pl.ds(pl.multiple_of(start, 2048), 2048)].reshape(16, 128)

    loads[0].wait()

    def pack_step(i, carry):
        psend[rows(i * 16, 16), :] = lanes((1 - core) * (CROWS * 128) + i * 2048)
        return carry

    lax.fori_loop(0, CROWS // 16, pack_step, 0, unroll=4)

    pl.semaphore_wait(barrier, len(peers))

    def at_y(ref, d, start=0, size=YROWS):
        return ref.at[rows(lax.rem(y + d, NY) * YROWS + start, size), :]

    order = (3, 5, 4, 1, 7, 2, 6, 0)
    for d in order:
        send(at_y(psend, d), at_y(precv, d), partner, "pair", d)
    loads[1].wait()
    send(cot.at[0], cot.at[1], to_x(1), "c", 1)
    send(cot.at[0], cot.at[3], to_x(-1), "c", -1)

    loads[2].wait()
    loads[3].wait()
    diag = lax.broadcasted_iota(jnp.int32, (ROWS, ROWS), 0) == lax.broadcasted_iota(jnp.int32, (ROWS, ROWS), 1)
    gain_row = gain[...].astype(BF16).astype(F32)
    gain_col = jnp.sum(jnp.where(diag, gain_row, 0.0), axis=1, keepdims=True)

    def wrows(zz):
        return wx.at[rows(zz * ROWS, ROWS), :]

    wrows(zl)[...] = (w[...].astype(F32) * gain_col).astype(BF16)
    for d in range(1, NZL):
        send(wrows(zl), wrows(zl), to_zl(d), "wz", d)

    for d in order:
        arrived(at_y(precv, d), "pair", d)
        base = lax.rem(y + d, NY) * YROWS

        def sum_step(i, carry, base=base):
            at = rows(base + i * 16, 16)
            own = lanes(core * (CROWS * 128) + (base + i * 16) * 128)
            hsum[at, :] = (own.astype(F32) + precv[at, :].astype(F32)).astype(BF16)
            return carry

        lax.fori_loop(0, YROWS // 16, sum_step, 0, unroll=4)
        if d == 3:
            send(at_y(hsum, 3), ya.at[0], to_y(1), "ya", 1)
        if d == 5:
            send(at_y(hsum, 5), ya.at[1], to_y(7), "ya", -1)
        if d == 4:
            send(at_y(hsum, 4, 0, YHALF), yb.at[0], to_y(2), "yb", 1)
            send(at_y(hsum, 4, YHALF, YHALF), yb.at[1], to_y(6), "yb", -1)
        if d == 1:
            send(at_y(hsum, 1), yc.at[0], to_y(1), "yc", 1)
        if d == 7:
            send(at_y(hsum, 7), yc.at[1], to_y(7), "yc", -1)

    loads[4].wait()

    def norm_step(i, carry):
        at = rows(i * 16, 16)
        wide = act[at, :].astype(F32)
        inv = lax.rsqrt(jnp.sum(wide * wide, axis=1, keepdims=True) * (1.0 / FEAT) + norm_eps)
        xhat[at, :] = (wide * inv).astype(BF16)
        return carry

    lax.fori_loop(0, TOK // 16, norm_step, 0)

    for j in range(FEAT // 256):
        xt[j * 256:(j + 1) * 256, :] = xhat[:, j * 256:(j + 1) * 256].T

    right, left, far = lax.rem(x + 1, NX), lax.rem(x + 3, NX), lax.rem(x + 2, NX)

    def block(xx):
        return xt.at[rows(xx * XROWS, XROWS), :]

    def half(xx, h):
        return xt.at[rows(xx * XROWS + h * XHALF, XHALF), :]

    send(half(far, 0), relay.at[0], to_x(1), "r", 1)
    send(half(far, 1), relay.at[1], to_x(-1), "r", -1)
    send(block(right), xin.at[0], to_x(1), "x", 1)
    send(block(left), xin.at[2], to_x(-1), "x", -1)

    def combine(d, h, k, sign):
        arrived(ya.at[k], "ya", sign)
        arrived(yb.at[k], "yb", sign)
        near, other = at_y(hsum, d, h * YHALF, YHALF), at_y(hsum, d, (1 - h) * YHALF, YHALF)
        near[...] = (near[...].astype(F32) + ya[k, h * YHALF:(h + 1) * YHALF].astype(F32)
                     + yb[k].astype(F32)).astype(BF16)
        other[...] = (other[...].astype(F32)
                      + ya[k, (1 - h) * YHALF:(2 - h) * YHALF].astype(F32)).astype(BF16)
        send(at_y(hsum, d), yd.at[k], to_y(d), "yd", sign)

    combine(2, 0, 0, 1)
    combine(6, 1, 1, -1)

    arrived(relay.at[0], "r", 1)
    send(relay.at[0], xin.at[1, pl.ds(0, XHALF), :], to_x(1), "f", 1)
    arrived(relay.at[1], "r", -1)
    send(relay.at[1], xin.at[1, pl.ds(XHALF, XHALF), :], to_x(-1), "f", -1)
    arrived(cot.at[1], "c", 1)
    send(cot.at[1, pl.ds(0, THALF), :], cot.at[2, pl.ds(0, THALF), :], to_x(1), "d", 1)
    arrived(cot.at[3], "c", -1)
    send(cot.at[3, pl.ds(THALF, THALF), :], cot.at[2, pl.ds(THALF, THALF), :], to_x(-1), "d", -1)

    total = at_y(hsum, 0)[...].astype(F32)
    for k, sign in ((0, 1), (1, -1)):
        arrived(yc.at[k], "yc", sign)
        total = total + yc[k].astype(F32)
    for k, sign in ((0, 1), (1, -1)):
        arrived(yd.at[k], "yd", sign)
        total = total + yd[k].astype(F32)
    zall[zh] = total.astype(BF16)
    for d in range(1, NZH):
        send(zall.at[zh], zall.at[zh], to_zh(d), "z", d)

    for d in range(1, NZL):
        arrived(wrows(lax.rem(zl - d + NZL, NZL)), "wz", d)

    def partial_keys(ref):
        return lax.dot_general(ref[...], wx[...], (((0,), (0,)), ((), ())), preferred_element_type=F32)

    kown[...] = partial_keys(block(x))
    arrived(xin.at[0], "x", 1)
    kpart[0] = partial_keys(xin.at[0]).astype(BF16)
    arrived(xin.at[2], "x", -1)
    kpart[2] = partial_keys(xin.at[2]).astype(BF16)

    arrived(xin.at[1, pl.ds(0, XHALF), :], "f", 1)
    arrived(xin.at[1, pl.ds(XHALF, XHALF), :], "f", -1)
    kpart[1] = partial_keys(xin.at[1]).astype(BF16)
    send(kpart.at[1, pl.ds(0, THALF), :], kin1.at[0], to_x(1), "k1", 1)
    send(kpart.at[1, pl.ds(THALF, THALF), :], kin1.at[1], to_x(-1), "k1", -1)

    def chunk(d, cc, start=0, size=YROWS):
        return dbuf.at[rows(cc * CROWS + lax.rem(y + d, NY) * YROWS + start, size), :]

    for d in range(1, NZH):
        arrived(zall.at[lax.rem(zh - d + NZH, NZH)], "z", d)
    total = zall[0].astype(F32)
    for k in range(1, NZH):
        total = total + zall[k].astype(F32)
    own = chunk(0, core)
    own[...] = (total * (1.0 / NS)).astype(BF16)
    for d in (2, 6, 1, 7):
        send(own, own, to_y(d), "yg", d)
    send(own, own, partner, "cg", 0)

    arrived(cot.at[2, pl.ds(0, THALF), :], "d", 1)
    arrived(cot.at[2, pl.ds(THALF, THALF), :], "d", -1)

    def product(zz):
        at = rows(zz * ROWS, ROWS)
        out = jnp.dot(xt[rows(x * XROWS + zz * ROWS, ROWS), :], cot[0], preferred_element_type=F32)
        for d in range(1, NX):
            out = out + jnp.dot(xin[d - 1, at, :], cot[d], preferred_element_type=F32)
        return out

    for d in range(1, NZL):
        zsend[d - 1] = product(lax.rem(zl + d, NZL)).astype(BF16)
        send(zsend.at[d - 1], zrecv.at[d - 1], to_zl(d), "gz", d)

    arrived(kin1.at[0], "k1", 1)
    kpart[2, :THALF] = (kpart[2, :THALF].astype(F32) + kin1[0].astype(F32)).astype(BF16)
    send(kpart.at[2], kin2.at[0], to_x(1), "k2", 1)
    arrived(kin1.at[1], "k1", -1)
    kpart[0, THALF:] = (kpart[0, THALF:].astype(F32) + kin1[1].astype(F32)).astype(BF16)
    send(kpart.at[0], kin2.at[1], to_x(-1), "k2", -1)

    wgrad_ref[...] = product(zl)

    arrived(chunk(6, core), "yg", 2)
    send(chunk(6, core), chunk(6, core), to_y(1), "yh", 1)
    send(chunk(6, core, 0, YHALF), chunk(6, core, 0, YHALF), to_y(2), "yi", 1)
    arrived(chunk(2, core), "yg", 6)
    send(chunk(2, core), chunk(2, core), to_y(7), "yh", -1)
    send(chunk(2, core, YHALF, YHALF), chunk(2, core, YHALF, YHALF), to_y(6), "yi", -1)
    send(chunk(6, core), chunk(6, core), partner, "cg", 6)
    send(chunk(2, core), chunk(2, core), partner, "cg", 2)
    arrived(chunk(7, core), "yg", 1)
    send(chunk(7, core), chunk(7, core), partner, "cg", 7)
    arrived(chunk(1, core), "yg", 7)
    send(chunk(1, core), chunk(1, core), partner, "cg", 1)
    arrived(chunk(5, core), "yh", 1)
    send(chunk(5, core), chunk(5, core), partner, "cg", 5)
    arrived(chunk(3, core), "yh", -1)
    send(chunk(3, core), chunk(3, core), partner, "cg", 3)
    arrived(chunk(4, core, 0, YHALF), "yi", 1)
    arrived(chunk(4, core, YHALF, YHALF), "yi", -1)
    send(chunk(4, core), chunk(4, core), partner, "cg", 4)

    arrived(kin2.at[0], "k2", 1)
    arrived(kin2.at[1], "k2", -1)
    keys_ref[...] = (kown[...] + kin2[0].astype(F32) + kin2[1].astype(F32)).astype(BF16)

    for d in range(1, NZL):
        arrived(zrecv.at[d - 1], "gz", d)
    gsum = wgrad_ref[...] + zrecv[0].astype(F32) + zrecv[1].astype(F32)
    gain_grad = jnp.sum(gsum * w[...].astype(F32), axis=1, keepdims=True)
    wgrad_ref[...] = gsum * gain_col
    ggrad_ref[...] = jnp.sum(jnp.where(diag, gain_grad, 0.0), axis=0, keepdims=True)

    for d in range(NY):
        arrived(chunk(d, 1 - core), "cg", d)
    delta_ref[...] = dbuf[...]
    for copy in pending:
        copy.wait_send()


def exchange(activations, key_cot, key_weight, norm_gain, pseudo_grad):
    slots = Slots()
    count = 64

    def body(*refs):
        kernel(slots, *refs)
        assert len(slots.index) <= count

    hbm = pl.BlockSpec(memory_space=pl.ANY)
    vmem = pl.BlockSpec(memory_space=pltpu.VMEM)
    return pl.pallas_call(
        body,
        out_shape=(
            jax.ShapeDtypeStruct((TOK, KVW), BF16),
            jax.ShapeDtypeStruct((ROWS, KVW), F32),
            jax.ShapeDtypeStruct((1, ROWS), F32),
            jax.ShapeDtypeStruct((FROWS, 128), BF16),
        ),
        in_specs=[hbm] * 5,
        out_specs=(vmem,) * 4,
        scratch_shapes=[
            pltpu.VMEM((TOK, FEAT), BF16),
            pltpu.VMEM((ROWS, KVW), BF16),
            pltpu.VMEM((1, ROWS), F32),
            pltpu.VMEM((1, FROWS * 128), BF16),
            pltpu.VMEM((TOK, FEAT), BF16),
            pltpu.VMEM((FEAT, TOK), BF16),
            pltpu.VMEM((NX - 1, XROWS, TOK), BF16),
            pltpu.VMEM((2, XHALF, TOK), BF16),
            pltpu.VMEM((NX, TOK, KVW), BF16),
            pltpu.VMEM((XROWS, KVW), BF16),
            pltpu.VMEM((NX - 1, TOK, KVW), BF16),
            pltpu.VMEM((2, THALF, KVW), BF16),
            pltpu.VMEM((2, TOK, KVW), BF16),
            pltpu.VMEM((TOK, KVW), F32),
            pltpu.VMEM((NZL - 1, ROWS, KVW), BF16),
            pltpu.VMEM((NZL - 1, ROWS, KVW), BF16),
            pltpu.VMEM((CROWS, 128), BF16),
            pltpu.VMEM((CROWS, 128), BF16),
            pltpu.VMEM((CROWS, 128), BF16),
            pltpu.VMEM((2, YROWS, 128), BF16),
            pltpu.VMEM((2, YHALF, 128), BF16),
            pltpu.VMEM((2, YROWS, 128), BF16),
            pltpu.VMEM((2, YROWS, 128), BF16),
            pltpu.VMEM((NZH, YROWS, 128), BF16),
            pltpu.VMEM((FROWS, 128), BF16),
            pltpu.SemaphoreType.DMA((5,)),
            pltpu.SemaphoreType.DMA((count,)),
            pltpu.SemaphoreType.DMA((count,)),
        ],
        compiler_params=pltpu.CompilerParams(
            collective_id=0, has_side_effects=True, vmem_limit_bytes=56 << 20
        ),
    )(activations, key_cot, key_weight, norm_gain, pseudo_grad)


def adam_step(params, gradient, first_moment, second_moment):
    first_new = beta_one * first_moment + (1.0 - beta_one) * gradient
    second_new = beta_two * second_moment + (1.0 - beta_two) * gradient * gradient
    update = (
        first_new / corr_one / (jnp.sqrt(second_new / corr_two) + adam_eps) + weight_decay * params
    )
    return (params - learn_rate * update, first_new, second_new)


def per_device(
    activations,
    key_cot,
    key_weight,
    weight_first,
    weight_second,
    norm_gain,
    gain_first,
    gain_second,
    pseudo_grad,
    outer_params,
    outer_mom,
):
    keys, weight_grad, gain_grad, delta = exchange(
        activations, key_cot, key_weight, norm_gain, pseudo_grad
    )
    new_weight, new_first, new_second = adam_step(
        key_weight[0].astype(F32), weight_grad, weight_first[0], weight_second[0]
    )
    new_gain, new_gain_first, new_gain_second = adam_step(
        norm_gain, gain_grad, gain_first, gain_second
    )
    wide_delta = delta.astype(F32)
    new_mom = outer_beta * outer_mom.reshape(FROWS, 128) + wide_delta
    new_params = outer_params.reshape(FROWS, 128) - outer_rate * (wide_delta + outer_beta * new_mom)
    return (
        keys[None],
        new_weight.astype(BF16)[None],
        new_first[None],
        new_second[None],
        new_gain,
        new_gain_first,
        new_gain_second,
        new_params.reshape(-1),
        new_mom.reshape(-1),
    )


def solution(mesh):
    return jax.shard_map(
        per_device,
        mesh=mesh,
        in_specs=(
            P("silo", "fsdp", None),
            P("silo", "fsdp", None),
            P("silo", "fsdp", None),
            P("silo", "fsdp", None),
            P("silo", "fsdp", None),
            P("silo", "fsdp"),
            P("silo", "fsdp"),
            P("silo", "fsdp"),
            P("silo", "fsdp"),
            P("fsdp"),
            P("fsdp"),
        ),
        out_specs=(
            P("silo", "fsdp", None),
            P("silo", "fsdp", None),
            P("silo", "fsdp", None),
            P("silo", "fsdp", None),
            P("silo", "fsdp"),
            P("silo", "fsdp"),
            P("silo", "fsdp"),
            P("fsdp"),
            P("fsdp"),
        ),
        check_vma=False,
    )
```

```python
import math

import jax
import jax.numpy as jnp
from jax import lax
from jax.experimental import pallas as pl
from jax.experimental.pallas import tpu as pltpu
from jax.sharding import PartitionSpec as P

norm_eps = 1e-05
beta_one = 0.9
beta_two = 0.95
corr_one = 1.0 - math.exp(200.0 * math.log(0.9))
corr_two = 1.0 - math.exp(200.0 * math.log(0.95))
learn_rate = 0.001
adam_eps = 1e-08
weight_decay = 0.1
outer_beta = 0.9
outer_rate = 0.7

MESH = pl.DeviceIdType.MESH
NX, NZL = 4, 3
NY, NZH, NC = 8, 4, 2
NF, NS = NX * NZL, NY * NZH * NC
FEAT, KVW, TOK = 2304, 512, 256
ROWS = FEAT // NF
XROWS = FEAT // NX
XHALF = XROWS // 2
THALF = TOK // 2
FROWS = 3072
CROWS = FROWS // NC
YROWS = CROWS // NY
YHALF = YROWS // 2
F32, BF16 = jnp.float32, jnp.bfloat16


class Slots:
    def __init__(self):
        self.index = {}

    def __call__(self, *name):
        return self.index.setdefault(name, len(self.index))


def kernel(slots, act_hbm, cot_hbm, w_hbm, gain_hbm, pg_hbm, keys_out, wgrad_out, ggrad_out, delta_out,
           act, w, gain, pg, xhat, xt, xin, relay, cot, wx, kpart, kin1, kin2, kown, zsend, zrecv,
           psend, precv, hsum, ya, yb, yc, yd, zall, dbuf, keys_ref, wgrad_ref, ggrad_ref, lsem, ssem, rsem):
    s, f = lax.axis_index("silo"), lax.axis_index("fsdp")
    core = lax.rem(s, NC)
    zh = lax.rem(s // NC, NZH)
    y = s // (NC * NZH)
    x, zl = f // NZL, lax.rem(f, NZL)

    def silo_at(yy, zz, cc):
        return (yy * NZH + zz) * NC + cc

    def fsdp_at(xx, zz):
        return xx * NZL + zz

    def to_y(d):
        return {"silo": silo_at(lax.rem(y + d, NY), zh, core), "fsdp": f}

    def to_zh(d):
        return {"silo": silo_at(y, lax.rem(zh + d, NZH), core), "fsdp": f}

    def to_zl(d):
        return {"silo": s, "fsdp": fsdp_at(x, lax.rem(zl + d, NZL))}

    def to_x(d):
        return {"silo": s, "fsdp": fsdp_at(lax.rem(x + d + NX, NX), zl)}

    partner = {"silo": silo_at(y, zh, 1 - core), "fsdp": f}
    peers = ([to_y(d) for d in (1, 2, 6, 7)] + [to_zh(d) for d in range(1, NZH)]
             + [to_zl(d) for d in range(1, NZL)] + [to_x(1), to_x(-1)] + [partner])
    pending = []
    results = []

    def result(src, dst):
        copy = pltpu.make_async_copy(src, dst, lsem.at[len(loads) + len(results)])
        copy.start()
        results.append(copy)

    def remote(src, dst, device, *name):
        k = slots(*name)
        return pltpu.make_async_remote_copy(
            src_ref=src, dst_ref=dst, send_sem=ssem.at[k], recv_sem=rsem.at[k],
            device_id=device, device_id_type=MESH)

    def send(src, dst, device, *name):
        copy = remote(src, dst, device, *name)
        copy.start()
        pending.append(copy)

    def arrived(ref, *name):
        remote(ref, ref, partner, *name).wait_recv()

    barrier = pltpu.get_barrier_semaphore()
    for peer in peers:
        pl.semaphore_signal(barrier, inc=1, device_id=peer, device_id_type=MESH)

    loads = [pltpu.make_async_copy(a, b, lsem.at[i]) for i, (a, b) in enumerate((
        (pg_hbm, pg), (cot_hbm.at[0], cot.at[0]), (w_hbm.at[0], w), (gain_hbm, gain), (act_hbm.at[0], act)))]
    for load in loads:
        load.start()

    def rows(start, size):
        return pl.ds(pl.multiple_of(start, 16), size)

    def lanes(start):
        return pg[0, pl.ds(pl.multiple_of(start, 2048), 2048)].reshape(16, 128)

    loads[0].wait()

    def pack_step(i, carry):
        psend[rows(i * 16, 16), :] = lanes((1 - core) * (CROWS * 128) + i * 2048)
        return carry

    lax.fori_loop(0, CROWS // 16, pack_step, 0, unroll=4)

    pl.semaphore_wait(barrier, len(peers))

    def at_y(ref, d, start=0, size=YROWS):
        return ref.at[rows(lax.rem(y + d, NY) * YROWS + start, size), :]

    order = (3, 5, 4, 1, 7, 2, 6, 0)
    for d in order:
        send(at_y(psend, d), at_y(precv, d), partner, "pair", d)
    loads[1].wait()
    send(cot.at[0], cot.at[1], to_x(1), "c", 1)
    send(cot.at[0], cot.at[3], to_x(-1), "c", -1)

    loads[2].wait()
    loads[3].wait()
    diag = lax.broadcasted_iota(jnp.int32, (ROWS, ROWS), 0) == lax.broadcasted_iota(jnp.int32, (ROWS, ROWS), 1)
    gain_row = gain[...].astype(BF16).astype(F32)
    gain_col = jnp.sum(jnp.where(diag, gain_row, 0.0), axis=1, keepdims=True)

    def wrows(zz):
        return wx.at[rows(zz * ROWS, ROWS), :]

    wrows(zl)[...] = (w[...].astype(F32) * gain_col).astype(BF16)
    for d in range(1, NZL):
        send(wrows(zl), wrows(zl), to_zl(d), "wz", d)

    loads[4].wait()

    def norm_step(i, carry):
        at = rows(i * 16, 16)
        wide = act[at, :].astype(F32)
        inv = lax.rsqrt(jnp.sum(wide * wide, axis=1, keepdims=True) * (1.0 / FEAT) + norm_eps)
        xhat[at, :] = (wide * inv).astype(BF16)
        return carry

    lax.fori_loop(0, TOK // 16, norm_step, 0)

    for d in order:
        arrived(at_y(precv, d), "pair", d)
        base = lax.rem(y + d, NY) * YROWS

        def sum_step(i, carry, base=base):
            at = rows(base + i * 16, 16)
            own = lanes(core * (CROWS * 128) + (base + i * 16) * 128)
            hsum[at, :] = (own.astype(F32) + precv[at, :].astype(F32)).astype(BF16)
            return carry

        lax.fori_loop(0, YROWS // 16, sum_step, 0, unroll=4)
        if d == 3:
            send(at_y(hsum, 3), ya.at[0], to_y(1), "ya", 1)
        if d == 5:
            send(at_y(hsum, 5), ya.at[1], to_y(7), "ya", -1)
        if d == 4:
            send(at_y(hsum, 4, 0, YHALF), yb.at[0], to_y(2), "yb", 1)
            send(at_y(hsum, 4, YHALF, YHALF), yb.at[1], to_y(6), "yb", -1)
        if d == 1:
            send(at_y(hsum, 1), yc.at[0], to_y(1), "yc", 1)
        if d == 7:
            send(at_y(hsum, 7), yc.at[1], to_y(7), "yc", -1)

    for j in range(FEAT // 256):
        xt[j * 256:(j + 1) * 256, :] = xhat[:, j * 256:(j + 1) * 256].T

    right, left, far = lax.rem(x + 1, NX), lax.rem(x + 3, NX), lax.rem(x + 2, NX)

    def block(xx):
        return xt.at[rows(xx * XROWS, XROWS), :]

    def half(xx, h):
        return xt.at[rows(xx * XROWS + h * XHALF, XHALF), :]

    send(half(far, 0), relay.at[0], to_x(1), "r", 1)
    send(half(far, 1), relay.at[1], to_x(-1), "r", -1)
    send(block(right), xin.at[0], to_x(1), "x", 1)
    send(block(left), xin.at[2], to_x(-1), "x", -1)

    def combine(d, h, k, sign):
        arrived(ya.at[k], "ya", sign)
        arrived(yb.at[k], "yb", sign)
        near, other = at_y(hsum, d, h * YHALF, YHALF), at_y(hsum, d, (1 - h) * YHALF, YHALF)
        near[...] = (near[...].astype(F32) + ya[k, h * YHALF:(h + 1) * YHALF].astype(F32)
                     + yb[k].astype(F32)).astype(BF16)
        other[...] = (other[...].astype(F32)
                      + ya[k, (1 - h) * YHALF:(2 - h) * YHALF].astype(F32)).astype(BF16)
        send(at_y(hsum, d), yd.at[k], to_y(d), "yd", sign)

    combine(2, 0, 0, 1)
    combine(6, 1, 1, -1)

    arrived(relay.at[0], "r", 1)
    send(relay.at[0], xin.at[1, pl.ds(0, XHALF), :], to_x(1), "f", 1)
    arrived(relay.at[1], "r", -1)
    send(relay.at[1], xin.at[1, pl.ds(XHALF, XHALF), :], to_x(-1), "f", -1)
    arrived(cot.at[1], "c", 1)
    send(cot.at[1, pl.ds(0, THALF), :], cot.at[2, pl.ds(0, THALF), :], to_x(1), "d", 1)
    arrived(cot.at[3], "c", -1)
    send(cot.at[3, pl.ds(THALF, THALF), :], cot.at[2, pl.ds(THALF, THALF), :], to_x(-1), "d", -1)

    total = at_y(hsum, 0)[...].astype(F32)
    for k, sign in ((0, 1), (1, -1)):
        arrived(yc.at[k], "yc", sign)
        total = total + yc[k].astype(F32)
    for k, sign in ((0, 1), (1, -1)):
        arrived(yd.at[k], "yd", sign)
        total = total + yd[k].astype(F32)
    zall[zh] = total.astype(BF16)
    for d in range(1, NZH):
        send(zall.at[zh], zall.at[zh], to_zh(d), "z", d)

    for d in range(1, NZL):
        arrived(wrows(lax.rem(zl - d + NZL, NZL)), "wz", d)

    def partial_keys(ref):
        return lax.dot_general(ref[...], wx[...], (((0,), (0,)), ((), ())), preferred_element_type=F32)

    kown[...] = partial_keys(block(x))
    arrived(xin.at[0], "x", 1)
    kpart[0] = partial_keys(xin.at[0]).astype(BF16)
    arrived(xin.at[2], "x", -1)
    kpart[2] = partial_keys(xin.at[2]).astype(BF16)

    arrived(xin.at[1, pl.ds(0, XHALF), :], "f", 1)
    arrived(xin.at[1, pl.ds(XHALF, XHALF), :], "f", -1)
    kpart[1] = partial_keys(xin.at[1]).astype(BF16)
    send(kpart.at[1, pl.ds(0, THALF), :], kin1.at[0], to_x(1), "k1", 1)
    send(kpart.at[1, pl.ds(THALF, THALF), :], kin1.at[1], to_x(-1), "k1", -1)

    def chunk(d, cc, start=0, size=YROWS):
        return dbuf.at[rows(cc * CROWS + lax.rem(y + d, NY) * YROWS + start, size), :]

    for d in range(1, NZH):
        arrived(zall.at[lax.rem(zh - d + NZH, NZH)], "z", d)
    total = zall[0].astype(F32)
    for k in range(1, NZH):
        total = total + zall[k].astype(F32)
    def deliver(d, cc):
        at = rows(cc * CROWS + lax.rem(y + d, NY) * YROWS, YROWS)
        result(dbuf.at[at, :], delta_out.at[at, :])

    own = chunk(0, core)
    own[...] = (total * (1.0 / NS)).astype(BF16)
    for d in (2, 6, 1, 7):
        send(own, own, to_y(d), "yg", d)
    send(own, own, partner, "cg", 0)
    deliver(0, core)

    arrived(cot.at[2, pl.ds(0, THALF), :], "d", 1)
    arrived(cot.at[2, pl.ds(THALF, THALF), :], "d", -1)

    def product(zz):
        at = rows(zz * ROWS, ROWS)
        out = jnp.dot(xt[rows(x * XROWS + zz * ROWS, ROWS), :], cot[0], preferred_element_type=F32)
        for d in range(1, NX):
            out = out + jnp.dot(xin[d - 1, at, :], cot[d], preferred_element_type=F32)
        return out

    for d in range(1, NZL):
        zsend[d - 1] = product(lax.rem(zl + d, NZL)).astype(BF16)
        send(zsend.at[d - 1], zrecv.at[d - 1], to_zl(d), "gz", d)

    arrived(kin1.at[0], "k1", 1)
    kpart[2, :THALF] = (kpart[2, :THALF].astype(F32) + kin1[0].astype(F32)).astype(BF16)
    send(kpart.at[2], kin2.at[0], to_x(1), "k2", 1)
    arrived(kin1.at[1], "k1", -1)
    kpart[0, THALF:] = (kpart[0, THALF:].astype(F32) + kin1[1].astype(F32)).astype(BF16)
    send(kpart.at[0], kin2.at[1], to_x(-1), "k2", -1)

    wgrad_ref[...] = product(zl)

    arrived(chunk(6, core), "yg", 2)
    send(chunk(6, core), chunk(6, core), to_y(1), "yh", 1)
    send(chunk(6, core, 0, YHALF), chunk(6, core, 0, YHALF), to_y(2), "yi", 1)
    arrived(chunk(2, core), "yg", 6)
    send(chunk(2, core), chunk(2, core), to_y(7), "yh", -1)
    send(chunk(2, core, YHALF, YHALF), chunk(2, core, YHALF, YHALF), to_y(6), "yi", -1)
    send(chunk(6, core), chunk(6, core), partner, "cg", 6)
    deliver(6, core)
    send(chunk(2, core), chunk(2, core), partner, "cg", 2)
    deliver(2, core)
    arrived(chunk(7, core), "yg", 1)
    send(chunk(7, core), chunk(7, core), partner, "cg", 7)
    deliver(7, core)
    arrived(chunk(1, core), "yg", 7)
    send(chunk(1, core), chunk(1, core), partner, "cg", 1)
    deliver(1, core)
    arrived(chunk(5, core), "yh", 1)
    send(chunk(5, core), chunk(5, core), partner, "cg", 5)
    deliver(5, core)
    arrived(chunk(3, core), "yh", -1)
    send(chunk(3, core), chunk(3, core), partner, "cg", 3)
    deliver(3, core)
    arrived(chunk(4, core, 0, YHALF), "yi", 1)
    arrived(chunk(4, core, YHALF, YHALF), "yi", -1)
    send(chunk(4, core), chunk(4, core), partner, "cg", 4)
    deliver(4, core)

    arrived(kin2.at[0], "k2", 1)
    arrived(kin2.at[1], "k2", -1)
    keys_ref[...] = (kown[...] + kin2[0].astype(F32) + kin2[1].astype(F32)).astype(BF16)
    result(keys_ref, keys_out)

    for d in range(1, NZL):
        arrived(zrecv.at[d - 1], "gz", d)
    gsum = wgrad_ref[...] + zrecv[0].astype(F32) + zrecv[1].astype(F32)
    gain_grad = jnp.sum(gsum * w[...].astype(F32), axis=1, keepdims=True)
    wgrad_ref[...] = gsum * gain_col
    ggrad_ref[...] = jnp.sum(jnp.where(diag, gain_grad, 0.0), axis=0, keepdims=True)

    result(wgrad_ref, wgrad_out)
    result(ggrad_ref, ggrad_out)

    for d in (0, 6, 2, 7, 1, 5, 3, 4):
        arrived(chunk(d, 1 - core), "cg", d)
        deliver(d, 1 - core)
    for copy in pending:
        copy.wait_send()
    for copy in results:
        copy.wait()


def exchange(activations, key_cot, key_weight, norm_gain, pseudo_grad):
    slots = Slots()
    count = 64

    def body(*refs):
        kernel(slots, *refs)
        assert len(slots.index) <= count

    hbm = pl.BlockSpec(memory_space=pl.ANY)
    return pl.pallas_call(
        body,
        out_shape=(
            jax.ShapeDtypeStruct((TOK, KVW), BF16),
            jax.ShapeDtypeStruct((ROWS, KVW), F32),
            jax.ShapeDtypeStruct((1, ROWS), F32),
            jax.ShapeDtypeStruct((FROWS, 128), BF16),
        ),
        in_specs=[hbm] * 5,
        out_specs=(hbm,) * 4,
        scratch_shapes=[
            pltpu.VMEM((TOK, FEAT), BF16),
            pltpu.VMEM((ROWS, KVW), BF16),
            pltpu.VMEM((1, ROWS), F32),
            pltpu.VMEM((1, FROWS * 128), BF16),
            pltpu.VMEM((TOK, FEAT), BF16),
            pltpu.VMEM((FEAT, TOK), BF16),
            pltpu.VMEM((NX - 1, XROWS, TOK), BF16),
            pltpu.VMEM((2, XHALF, TOK), BF16),
            pltpu.VMEM((NX, TOK, KVW), BF16),
            pltpu.VMEM((XROWS, KVW), BF16),
            pltpu.VMEM((NX - 1, TOK, KVW), BF16),
            pltpu.VMEM((2, THALF, KVW), BF16),
            pltpu.VMEM((2, TOK, KVW), BF16),
            pltpu.VMEM((TOK, KVW), F32),
            pltpu.VMEM((NZL - 1, ROWS, KVW), BF16),
            pltpu.VMEM((NZL - 1, ROWS, KVW), BF16),
            pltpu.VMEM((CROWS, 128), BF16),
            pltpu.VMEM((CROWS, 128), BF16),
            pltpu.VMEM((CROWS, 128), BF16),
            pltpu.VMEM((2, YROWS, 128), BF16),
            pltpu.VMEM((2, YHALF, 128), BF16),
            pltpu.VMEM((2, YROWS, 128), BF16),
            pltpu.VMEM((2, YROWS, 128), BF16),
            pltpu.VMEM((NZH, YROWS, 128), BF16),
            pltpu.VMEM((FROWS, 128), BF16),
            pltpu.VMEM((TOK, KVW), BF16),
            pltpu.VMEM((ROWS, KVW), F32),
            pltpu.VMEM((1, ROWS), F32),
            pltpu.SemaphoreType.DMA((5 + 3 + 2 * NY,)),
            pltpu.SemaphoreType.DMA((count,)),
            pltpu.SemaphoreType.DMA((count,)),
        ],
        compiler_params=pltpu.CompilerParams(
            collective_id=0, has_side_effects=True, vmem_limit_bytes=56 << 20
        ),
    )(activations, key_cot, key_weight, norm_gain, pseudo_grad)


def adam_step(params, gradient, first_moment, second_moment):
    first_new = beta_one * first_moment + (1.0 - beta_one) * gradient
    second_new = beta_two * second_moment + (1.0 - beta_two) * gradient * gradient
    update = (
        first_new / corr_one / (jnp.sqrt(second_new / corr_two) + adam_eps) + weight_decay * params
    )
    return (params - learn_rate * update, first_new, second_new)


PARTS = 4


def update_kernel(*refs):
    ins, outs, (stage_in, stage_out, sems) = refs[:12], refs[12:21], refs[21:]
    keys, wgrad, ggrad, delta, weight, first, second, gain, gain_first, gain_second, params, mom = stage_in
    started = []

    def copy(src, dst):
        c = pltpu.make_async_copy(src, dst, sems.at[len(started)])
        c.start()
        started.append(c)
        return c

    part = FROWS // PARTS
    pieces = [slice(k * part, (k + 1) * part) for k in range(PARTS)]
    outer_in = []
    for at in pieces:
        outer_in.append([copy(ins[k].at[at, :], stage_in[k].at[at, :]) for k in (3, 10, 11)])
    adam_in = [copy(ins[k], stage_in[k]) for k in (1, 4, 5, 6)]
    gain_in = [copy(ins[k], stage_in[k]) for k in (2, 7, 8, 9)]
    keys_in = copy(ins[0], keys)
    done = []
    for at, waits in zip(pieces, outer_in):
        for c in waits:
            c.wait()
        wide = delta[at, :].astype(F32)
        new_mom = outer_beta * mom[at, :] + wide
        stage_out[7][at, :] = new_mom
        stage_out[6][at, :] = params[at, :] - outer_rate * (wide + outer_beta * new_mom)
        done.append(copy(stage_out[6].at[at, :], outs[7].at[at, :]))
        done.append(copy(stage_out[7].at[at, :], outs[8].at[at, :]))
    keys_in.wait()
    done.append(copy(keys, outs[0]))
    for c in adam_in:
        c.wait()
    new_weight, new_first, new_second = adam_step(
        weight[0].astype(F32), wgrad[...], first[0], second[0]
    )
    stage_out[0][0] = new_weight.astype(BF16)
    stage_out[1][0] = new_first
    stage_out[2][0] = new_second
    for k in range(3):
        done.append(copy(stage_out[k], outs[1 + k]))
    for c in gain_in:
        c.wait()
    for k, value in enumerate(adam_step(gain[...], ggrad[...], gain_first[...], gain_second[...])):
        stage_out[3 + k][...] = value
        done.append(copy(stage_out[3 + k], outs[4 + k]))
    for c in done:
        c.wait()


def update(*arrays):
    hbm = pl.BlockSpec(memory_space=pl.ANY)
    weights, gains, outer = (1, ROWS, KVW), (1, ROWS), (FROWS, 128)
    kinds = (
        ((TOK, KVW), BF16), (weights, BF16), (weights, F32), (weights, F32),
        (gains, F32), (gains, F32), (gains, F32), (outer, F32), (outer, F32),
    )
    return pl.pallas_call(
        update_kernel,
        out_shape=tuple(jax.ShapeDtypeStruct(*kind) for kind in kinds),
        in_specs=[hbm] * 12,
        out_specs=(hbm,) * 9,
        scratch_shapes=[
            tuple(pltpu.VMEM(a.shape, a.dtype) for a in arrays),
            tuple(pltpu.VMEM(*kind) for kind in kinds[1:]),
            pltpu.SemaphoreType.DMA((3 * PARTS + 9 + 2 * PARTS + 7,)),
        ],
        compiler_params=pltpu.CompilerParams(vmem_limit_bytes=56 << 20),
    )(*arrays)


def per_device(
    activations,
    key_cot,
    key_weight,
    weight_first,
    weight_second,
    norm_gain,
    gain_first,
    gain_second,
    pseudo_grad,
    outer_params,
    outer_mom,
):
    keys, weight_grad, gain_grad, delta = exchange(
        activations, key_cot, key_weight, norm_gain, pseudo_grad
    )
    (keys, new_weight, new_first, new_second, new_gain, new_gain_first, new_gain_second, new_params,
     new_mom) = update(
        keys, weight_grad, gain_grad, delta, key_weight, weight_first, weight_second, norm_gain,
        gain_first, gain_second, outer_params.reshape(FROWS, 128), outer_mom.reshape(FROWS, 128),
    )
    return (
        keys[None],
        new_weight,
        new_first,
        new_second,
        new_gain,
        new_gain_first,
        new_gain_second,
        new_params.reshape(-1),
        new_mom.reshape(-1),
    )


def solution(mesh):
    return jax.shard_map(
        per_device,
        mesh=mesh,
        in_specs=(
            P("silo", "fsdp", None),
            P("silo", "fsdp", None),
            P("silo", "fsdp", None),
            P("silo", "fsdp", None),
            P("silo", "fsdp", None),
            P("silo", "fsdp"),
            P("silo", "fsdp"),
            P("silo", "fsdp"),
            P("silo", "fsdp"),
            P("fsdp"),
            P("fsdp"),
        ),
        out_specs=(
            P("silo", "fsdp", None),
            P("silo", "fsdp", None),
            P("silo", "fsdp", None),
            P("silo", "fsdp", None),
            P("silo", "fsdp"),
            P("silo", "fsdp"),
            P("silo", "fsdp"),
            P("fsdp"),
            P("fsdp"),
        ),
        check_vma=False,
    )
```

```python
import math

import jax
import jax.numpy as jnp
from jax import lax
from jax.experimental import pallas as pl
from jax.experimental.pallas import tpu as pltpu
from jax.sharding import PartitionSpec as P

norm_eps = 1e-05
beta_one = 0.9
beta_two = 0.95
corr_one = 1.0 - math.exp(200.0 * math.log(0.9))
corr_two = 1.0 - math.exp(200.0 * math.log(0.95))
learn_rate = 0.001
adam_eps = 1e-08
weight_decay = 0.1
outer_beta = 0.9
outer_rate = 0.7

MESH = pl.DeviceIdType.MESH
NX, NZL = 4, 3
NY, NZH, NC = 8, 4, 2
NF, NS = NX * NZL, NY * NZH * NC
FEAT, KVW, TOK = 2304, 512, 256
ROWS = FEAT // NF
XROWS = FEAT // NX
XHALF = XROWS // 2
THALF = TOK // 2
FROWS = 3072
CROWS = FROWS // NC
YROWS = CROWS // NY
YHALF = YROWS // 2
F32, BF16 = jnp.float32, jnp.bfloat16


class Slots:
    def __init__(self):
        self.index = {}

    def __call__(self, *name):
        return self.index.setdefault(name, len(self.index))


def kernel(slots, act_hbm, cot_hbm, w_hbm, gain_hbm, pg_hbm, keys_out, wgrad_out, ggrad_out, delta_out,
           act, w, gain, pg, xhat, xt, xin, relay, cot, wx, kpart, kin1, kin2, kown, zsend, zrecv,
           psend, precv, hsum, ya, yb, yc, yd, zall, dbuf, keys_ref, wgrad_ref, ggrad_ref, lsem, ssem, rsem):
    s, f = lax.axis_index("silo"), lax.axis_index("fsdp")
    core = lax.rem(s, NC)
    zh = lax.rem(s // NC, NZH)
    y = s // (NC * NZH)
    x, zl = f // NZL, lax.rem(f, NZL)

    def silo_at(yy, zz, cc):
        return (yy * NZH + zz) * NC + cc

    def fsdp_at(xx, zz):
        return xx * NZL + zz

    def to_y(d):
        return {"silo": silo_at(lax.rem(y + d, NY), zh, core), "fsdp": f}

    def to_zh(d):
        return {"silo": silo_at(y, lax.rem(zh + d, NZH), core), "fsdp": f}

    def to_zl(d):
        return {"silo": s, "fsdp": fsdp_at(x, lax.rem(zl + d, NZL))}

    def to_x(d):
        return {"silo": s, "fsdp": fsdp_at(lax.rem(x + d + NX, NX), zl)}

    partner = {"silo": silo_at(y, zh, 1 - core), "fsdp": f}
    peers = ([to_y(d) for d in (1, 2, 6, 7)] + [to_zh(d) for d in range(1, NZH)]
             + [to_zl(d) for d in range(1, NZL)] + [to_x(1), to_x(-1)] + [partner])
    pending = []
    results = []

    def result(src, dst):
        copy = pltpu.make_async_copy(src, dst, lsem.at[len(loads) + len(results)])
        copy.start()
        results.append(copy)

    def remote(src, dst, device, *name):
        k = slots(*name)
        return pltpu.make_async_remote_copy(
            src_ref=src, dst_ref=dst, send_sem=ssem.at[k], recv_sem=rsem.at[k],
            device_id=device, device_id_type=MESH)

    def send(src, dst, device, *name):
        copy = remote(src, dst, device, *name)
        copy.start()
        pending.append(copy)

    def arrived(ref, *name):
        remote(ref, ref, partner, *name).wait_recv()

    barrier = pltpu.get_barrier_semaphore()
    for peer in peers:
        pl.semaphore_signal(barrier, inc=1, device_id=peer, device_id_type=MESH)

    loads = [pltpu.make_async_copy(a, b, lsem.at[i]) for i, (a, b) in enumerate((
        (pg_hbm, pg), (cot_hbm.at[0], cot.at[0]), (w_hbm.at[0], w), (gain_hbm, gain), (act_hbm.at[0], act)))]
    for load in loads:
        load.start()

    def rows(start, size):
        return pl.ds(pl.multiple_of(start, 16), size)

    def lanes(start):
        return pg[0, pl.ds(pl.multiple_of(start, 2048), 2048)].reshape(16, 128)

    loads[0].wait()

    def pack_step(i, carry):
        psend[rows(i * 16, 16), :] = lanes((1 - core) * (CROWS * 128) + i * 2048)
        return carry

    lax.fori_loop(0, CROWS // 16, pack_step, 0, unroll=4)

    pl.semaphore_wait(barrier, len(peers))

    def at_y(ref, d, start=0, size=YROWS):
        return ref.at[rows(lax.rem(y + d, NY) * YROWS + start, size), :]

    order = (3, 5, 4, 1, 7, 2, 6, 0)
    for d in order:
        send(at_y(psend, d), at_y(precv, d), partner, "pair", d)
    loads[1].wait()
    send(cot.at[0], cot.at[1], to_x(1), "c", 1)
    send(cot.at[0], cot.at[3], to_x(-1), "c", -1)

    loads[2].wait()
    loads[3].wait()
    diag = lax.broadcasted_iota(jnp.int32, (ROWS, ROWS), 0) == lax.broadcasted_iota(jnp.int32, (ROWS, ROWS), 1)
    gain_row = gain[...].astype(BF16).astype(F32)
    gain_col = jnp.sum(jnp.where(diag, gain_row, 0.0), axis=1, keepdims=True)

    def wrows(zz):
        return wx.at[rows(zz * ROWS, ROWS), :]

    wrows(zl)[...] = (w[...].astype(F32) * gain_col).astype(BF16)
    for d in range(1, NZL):
        send(wrows(zl), wrows(zl), to_zl(d), "wz", d)

    loads[4].wait()

    def norm_step(i, carry):
        at = rows(i * 16, 16)
        wide = act[at, :].astype(F32)
        inv = lax.rsqrt(jnp.sum(wide * wide, axis=1, keepdims=True) * (1.0 / FEAT) + norm_eps)
        xhat[at, :] = (wide * inv).astype(BF16)
        return carry

    lax.fori_loop(0, TOK // 16, norm_step, 0)

    def pair_sum(d):
        arrived(at_y(precv, d), "pair", d)
        base = lax.rem(y + d, NY) * YROWS

        def sum_step(i, carry, base=base):
            at = rows(base + i * 16, 16)
            own = lanes(core * (CROWS * 128) + (base + i * 16) * 128)
            hsum[at, :] = (own.astype(F32) + precv[at, :].astype(F32)).astype(BF16)
            return carry

        lax.fori_loop(0, YROWS // 16, sum_step, 0, unroll=4)
        if d == 3:
            send(at_y(hsum, 3), ya.at[0], to_y(1), "ya", 1)
        if d == 5:
            send(at_y(hsum, 5), ya.at[1], to_y(7), "ya", -1)
        if d == 4:
            send(at_y(hsum, 4, 0, YHALF), yb.at[0], to_y(2), "yb", 1)
            send(at_y(hsum, 4, YHALF, YHALF), yb.at[1], to_y(6), "yb", -1)
        if d == 1:
            send(at_y(hsum, 1), yc.at[0], to_y(1), "yc", 1)
        if d == 7:
            send(at_y(hsum, 7), yc.at[1], to_y(7), "yc", -1)

    for d in order[:3]:
        pair_sum(d)

    for j in range(FEAT // 256):
        xt[j * 256:(j + 1) * 256, :] = xhat[:, j * 256:(j + 1) * 256].T

    right, left, far = lax.rem(x + 1, NX), lax.rem(x + 3, NX), lax.rem(x + 2, NX)

    def block(xx):
        return xt.at[rows(xx * XROWS, XROWS), :]

    def half(xx, h):
        return xt.at[rows(xx * XROWS + h * XHALF, XHALF), :]

    def third(k, d):
        return xin.at[k, rows(lax.rem(zl + d, NZL) * ROWS, ROWS), :]

    def send_thirds(d):
        zz = lax.rem(zl + d, NZL)
        for xx, k, sign in ((right, 0, 1), (left, 2, -1)):
            send(xt.at[rows(xx * XROWS + zz * ROWS, ROWS), :], third(k, d), to_x(sign), "x", d, sign)

    send(half(far, 0), relay.at[0], to_x(1), "r", 1)
    send(half(far, 1), relay.at[1], to_x(-1), "r", -1)
    for d in order[3:]:
        pair_sum(d)
    arrived(cot.at[1], "c", 1)
    send(cot.at[1, pl.ds(0, THALF), :], cot.at[2, pl.ds(0, THALF), :], to_x(1), "d", 1)
    arrived(cot.at[3], "c", -1)
    send(cot.at[3, pl.ds(THALF, THALF), :], cot.at[2, pl.ds(THALF, THALF), :], to_x(-1), "d", -1)
    send_thirds(1)

    def combine(d, h, k, sign):
        arrived(ya.at[k], "ya", sign)
        arrived(yb.at[k], "yb", sign)
        near, other = at_y(hsum, d, h * YHALF, YHALF), at_y(hsum, d, (1 - h) * YHALF, YHALF)
        near[...] = (near[...].astype(F32) + ya[k, h * YHALF:(h + 1) * YHALF].astype(F32)
                     + yb[k].astype(F32)).astype(BF16)
        other[...] = (other[...].astype(F32)
                      + ya[k, (1 - h) * YHALF:(2 - h) * YHALF].astype(F32)).astype(BF16)
        send(at_y(hsum, d), yd.at[k], to_y(d), "yd", sign)

    combine(2, 0, 0, 1)
    combine(6, 1, 1, -1)

    arrived(relay.at[0], "r", 1)
    send(relay.at[0], xin.at[1, pl.ds(0, XHALF), :], to_x(1), "f", 1)
    arrived(relay.at[1], "r", -1)
    send(relay.at[1], xin.at[1, pl.ds(XHALF, XHALF), :], to_x(-1), "f", -1)
    send_thirds(2)
    send_thirds(0)

    total = at_y(hsum, 0)[...].astype(F32)
    for k, sign in ((0, 1), (1, -1)):
        arrived(yc.at[k], "yc", sign)
        total = total + yc[k].astype(F32)
    for k, sign in ((0, 1), (1, -1)):
        arrived(yd.at[k], "yd", sign)
        total = total + yd[k].astype(F32)
    zall[zh] = total.astype(BF16)
    for d in range(1, NZH):
        send(zall.at[zh], zall.at[zh], to_zh(d), "z", d)

    for d in range(1, NZL):
        arrived(wrows(lax.rem(zl - d + NZL, NZL)), "wz", d)

    def partial_keys(ref):
        return lax.dot_general(ref[...], wx[...], (((0,), (0,)), ((), ())), preferred_element_type=F32)

    kown[...] = partial_keys(block(x))
    arrived(xin.at[1, pl.ds(0, XHALF), :], "f", 1)
    arrived(xin.at[1, pl.ds(XHALF, XHALF), :], "f", -1)
    kpart[1] = partial_keys(xin.at[1]).astype(BF16)
    send(kpart.at[1, pl.ds(0, THALF), :], kin1.at[0], to_x(1), "k1", 1)
    send(kpart.at[1, pl.ds(THALF, THALF), :], kin1.at[1], to_x(-1), "k1", -1)

    arrived(cot.at[2, pl.ds(0, THALF), :], "d", 1)
    arrived(cot.at[2, pl.ds(THALF, THALF), :], "d", -1)

    def product(zz):
        at = rows(zz * ROWS, ROWS)
        out = jnp.dot(xt[rows(x * XROWS + zz * ROWS, ROWS), :], cot[0], preferred_element_type=F32)
        for d in range(1, NX):
            out = out + jnp.dot(xin[d - 1, at, :], cot[d], preferred_element_type=F32)
        return out

    for d in range(1, NZL):
        arrived(third(0, d), "x", d, 1)
        arrived(third(2, d), "x", d, -1)
        zsend[d - 1] = product(lax.rem(zl + d, NZL)).astype(BF16)
        send(zsend.at[d - 1], zrecv.at[d - 1], to_zl(d), "gz", d)

    def chunk(d, cc, start=0, size=YROWS):
        return dbuf.at[rows(cc * CROWS + lax.rem(y + d, NY) * YROWS + start, size), :]

    for d in range(1, NZH):
        arrived(zall.at[lax.rem(zh - d + NZH, NZH)], "z", d)
    total = zall[0].astype(F32)
    for k in range(1, NZH):
        total = total + zall[k].astype(F32)
    def deliver(d, cc):
        at = rows(cc * CROWS + lax.rem(y + d, NY) * YROWS, YROWS)
        result(dbuf.at[at, :], delta_out.at[at, :])

    own = chunk(0, core)
    own[...] = (total * (1.0 / NS)).astype(BF16)
    for d in (2, 6, 1, 7):
        send(own, own, to_y(d), "yg", d)
    send(own, own, partner, "cg", 0)
    deliver(0, core)

    arrived(third(0, 0), "x", 0, 1)
    kpart[0] = partial_keys(xin.at[0]).astype(BF16)
    arrived(third(2, 0), "x", 0, -1)
    kpart[2] = partial_keys(xin.at[2]).astype(BF16)

    arrived(kin1.at[0], "k1", 1)
    kpart[2, :THALF] = (kpart[2, :THALF].astype(F32) + kin1[0].astype(F32)).astype(BF16)
    send(kpart.at[2], kin2.at[0], to_x(1), "k2", 1)
    arrived(kin1.at[1], "k1", -1)
    kpart[0, THALF:] = (kpart[0, THALF:].astype(F32) + kin1[1].astype(F32)).astype(BF16)
    send(kpart.at[0], kin2.at[1], to_x(-1), "k2", -1)

    wgrad_ref[...] = product(zl)

    arrived(chunk(6, core), "yg", 2)
    send(chunk(6, core), chunk(6, core), to_y(1), "yh", 1)
    send(chunk(6, core, 0, YHALF), chunk(6, core, 0, YHALF), to_y(2), "yi", 1)
    arrived(chunk(2, core), "yg", 6)
    send(chunk(2, core), chunk(2, core), to_y(7), "yh", -1)
    send(chunk(2, core, YHALF, YHALF), chunk(2, core, YHALF, YHALF), to_y(6), "yi", -1)
    send(chunk(6, core), chunk(6, core), partner, "cg", 6)
    deliver(6, core)
    send(chunk(2, core), chunk(2, core), partner, "cg", 2)
    deliver(2, core)
    arrived(chunk(7, core), "yg", 1)
    send(chunk(7, core), chunk(7, core), partner, "cg", 7)
    deliver(7, core)
    arrived(chunk(1, core), "yg", 7)
    send(chunk(1, core), chunk(1, core), partner, "cg", 1)
    deliver(1, core)
    arrived(chunk(5, core), "yh", 1)
    send(chunk(5, core), chunk(5, core), partner, "cg", 5)
    deliver(5, core)
    arrived(chunk(3, core), "yh", -1)
    send(chunk(3, core), chunk(3, core), partner, "cg", 3)
    deliver(3, core)
    arrived(chunk(4, core, 0, YHALF), "yi", 1)
    arrived(chunk(4, core, YHALF, YHALF), "yi", -1)
    send(chunk(4, core), chunk(4, core), partner, "cg", 4)
    deliver(4, core)

    arrived(kin2.at[0], "k2", 1)
    arrived(kin2.at[1], "k2", -1)
    keys_ref[...] = (kown[...] + kin2[0].astype(F32) + kin2[1].astype(F32)).astype(BF16)
    result(keys_ref, keys_out)

    for d in range(1, NZL):
        arrived(zrecv.at[d - 1], "gz", d)
    gsum = wgrad_ref[...] + zrecv[0].astype(F32) + zrecv[1].astype(F32)
    gain_grad = jnp.sum(gsum * w[...].astype(F32), axis=1, keepdims=True)
    wgrad_ref[...] = gsum * gain_col
    ggrad_ref[...] = jnp.sum(jnp.where(diag, gain_grad, 0.0), axis=0, keepdims=True)

    result(wgrad_ref, wgrad_out)
    result(ggrad_ref, ggrad_out)

    for d in (0, 6, 2, 7, 1, 5, 3, 4):
        arrived(chunk(d, 1 - core), "cg", d)
        deliver(d, 1 - core)
    for copy in pending:
        copy.wait_send()
    for copy in results:
        copy.wait()


def exchange(activations, key_cot, key_weight, norm_gain, pseudo_grad):
    slots = Slots()
    count = 64

    def body(*refs):
        kernel(slots, *refs)
        assert len(slots.index) <= count

    hbm = pl.BlockSpec(memory_space=pl.ANY)
    return pl.pallas_call(
        body,
        out_shape=(
            jax.ShapeDtypeStruct((TOK, KVW), BF16),
            jax.ShapeDtypeStruct((ROWS, KVW), F32),
            jax.ShapeDtypeStruct((1, ROWS), F32),
            jax.ShapeDtypeStruct((FROWS, 128), BF16),
        ),
        in_specs=[hbm] * 5,
        out_specs=(hbm,) * 4,
        scratch_shapes=[
            pltpu.VMEM((TOK, FEAT), BF16),
            pltpu.VMEM((ROWS, KVW), BF16),
            pltpu.VMEM((1, ROWS), F32),
            pltpu.VMEM((1, FROWS * 128), BF16),
            pltpu.VMEM((TOK, FEAT), BF16),
            pltpu.VMEM((FEAT, TOK), BF16),
            pltpu.VMEM((NX - 1, XROWS, TOK), BF16),
            pltpu.VMEM((2, XHALF, TOK), BF16),
            pltpu.VMEM((NX, TOK, KVW), BF16),
            pltpu.VMEM((XROWS, KVW), BF16),
            pltpu.VMEM((NX - 1, TOK, KVW), BF16),
            pltpu.VMEM((2, THALF, KVW), BF16),
            pltpu.VMEM((2, TOK, KVW), BF16),
            pltpu.VMEM((TOK, KVW), F32),
            pltpu.VMEM((NZL - 1, ROWS, KVW), BF16),
            pltpu.VMEM((NZL - 1, ROWS, KVW), BF16),
            pltpu.VMEM((CROWS, 128), BF16),
            pltpu.VMEM((CROWS, 128), BF16),
            pltpu.VMEM((CROWS, 128), BF16),
            pltpu.VMEM((2, YROWS, 128), BF16),
            pltpu.VMEM((2, YHALF, 128), BF16),
            pltpu.VMEM((2, YROWS, 128), BF16),
            pltpu.VMEM((2, YROWS, 128), BF16),
            pltpu.VMEM((NZH, YROWS, 128), BF16),
            pltpu.VMEM((FROWS, 128), BF16),
            pltpu.VMEM((TOK, KVW), BF16),
            pltpu.VMEM((ROWS, KVW), F32),
            pltpu.VMEM((1, ROWS), F32),
            pltpu.SemaphoreType.DMA((5 + 3 + 2 * NY,)),
            pltpu.SemaphoreType.DMA((count,)),
            pltpu.SemaphoreType.DMA((count,)),
        ],
        compiler_params=pltpu.CompilerParams(
            collective_id=0, has_side_effects=True, vmem_limit_bytes=56 << 20
        ),
    )(activations, key_cot, key_weight, norm_gain, pseudo_grad)


def adam_step(params, gradient, first_moment, second_moment):
    first_new = beta_one * first_moment + (1.0 - beta_one) * gradient
    second_new = beta_two * second_moment + (1.0 - beta_two) * gradient * gradient
    update = (
        first_new / corr_one / (jnp.sqrt(second_new / corr_two) + adam_eps) + weight_decay * params
    )
    return (params - learn_rate * update, first_new, second_new)


PARTS = 4


def update_kernel(*refs):
    ins, outs, (stage_in, stage_out, sems) = refs[:12], refs[12:21], refs[21:]
    keys, wgrad, ggrad, delta, weight, first, second, gain, gain_first, gain_second, params, mom = stage_in
    started = []

    def copy(src, dst):
        c = pltpu.make_async_copy(src, dst, sems.at[len(started)])
        c.start()
        started.append(c)
        return c

    part = FROWS // PARTS
    pieces = [slice(k * part, (k + 1) * part) for k in range(PARTS)]
    outer_in = []
    for at in pieces:
        outer_in.append([copy(ins[k].at[at, :], stage_in[k].at[at, :]) for k in (3, 10, 11)])
    adam_in = [copy(ins[k], stage_in[k]) for k in (1, 4, 5, 6)]
    gain_in = [copy(ins[k], stage_in[k]) for k in (2, 7, 8, 9)]
    keys_in = copy(ins[0], keys)
    done = []
    for at, waits in zip(pieces, outer_in):
        for c in waits:
            c.wait()
        wide = delta[at, :].astype(F32)
        new_mom = outer_beta * mom[at, :] + wide
        stage_out[7][at, :] = new_mom
        stage_out[6][at, :] = params[at, :] - outer_rate * (wide + outer_beta * new_mom)
        done.append(copy(stage_out[6].at[at, :], outs[7].at[at, :]))
        done.append(copy(stage_out[7].at[at, :], outs[8].at[at, :]))
    keys_in.wait()
    done.append(copy(keys, outs[0]))
    for c in adam_in:
        c.wait()
    new_weight, new_first, new_second = adam_step(
        weight[0].astype(F32), wgrad[...], first[0], second[0]
    )
    stage_out[0][0] = new_weight.astype(BF16)
    stage_out[1][0] = new_first
    stage_out[2][0] = new_second
    for k in range(3):
        done.append(copy(stage_out[k], outs[1 + k]))
    for c in gain_in:
        c.wait()
    for k, value in enumerate(adam_step(gain[...], ggrad[...], gain_first[...], gain_second[...])):
        stage_out[3 + k][...] = value
        done.append(copy(stage_out[3 + k], outs[4 + k]))
    for c in done:
        c.wait()


def update(*arrays):
    hbm = pl.BlockSpec(memory_space=pl.ANY)
    weights, gains, outer = (1, ROWS, KVW), (1, ROWS), (FROWS, 128)
    kinds = (
        ((TOK, KVW), BF16), (weights, BF16), (weights, F32), (weights, F32),
        (gains, F32), (gains, F32), (gains, F32), (outer, F32), (outer, F32),
    )
    return pl.pallas_call(
        update_kernel,
        out_shape=tuple(jax.ShapeDtypeStruct(*kind) for kind in kinds),
        in_specs=[hbm] * 12,
        out_specs=(hbm,) * 9,
        scratch_shapes=[
            tuple(pltpu.VMEM(a.shape, a.dtype) for a in arrays),
            tuple(pltpu.VMEM(*kind) for kind in kinds[1:]),
            pltpu.SemaphoreType.DMA((3 * PARTS + 9 + 2 * PARTS + 7,)),
        ],
        compiler_params=pltpu.CompilerParams(vmem_limit_bytes=56 << 20),
    )(*arrays)


def per_device(
    activations,
    key_cot,
    key_weight,
    weight_first,
    weight_second,
    norm_gain,
    gain_first,
    gain_second,
    pseudo_grad,
    outer_params,
    outer_mom,
):
    keys, weight_grad, gain_grad, delta = exchange(
        activations, key_cot, key_weight, norm_gain, pseudo_grad
    )
    (keys, new_weight, new_first, new_second, new_gain, new_gain_first, new_gain_second, new_params,
     new_mom) = update(
        keys, weight_grad, gain_grad, delta, key_weight, weight_first, weight_second, norm_gain,
        gain_first, gain_second, outer_params.reshape(FROWS, 128), outer_mom.reshape(FROWS, 128),
    )
    return (
        keys[None],
        new_weight,
        new_first,
        new_second,
        new_gain,
        new_gain_first,
        new_gain_second,
        new_params.reshape(-1),
        new_mom.reshape(-1),
    )


def solution(mesh):
    return jax.shard_map(
        per_device,
        mesh=mesh,
        in_specs=(
            P("silo", "fsdp", None),
            P("silo", "fsdp", None),
            P("silo", "fsdp", None),
            P("silo", "fsdp", None),
            P("silo", "fsdp", None),
            P("silo", "fsdp"),
            P("silo", "fsdp"),
            P("silo", "fsdp"),
            P("silo", "fsdp"),
            P("fsdp"),
            P("fsdp"),
        ),
        out_specs=(
            P("silo", "fsdp", None),
            P("silo", "fsdp", None),
            P("silo", "fsdp", None),
            P("silo", "fsdp", None),
            P("silo", "fsdp"),
            P("silo", "fsdp"),
            P("silo", "fsdp"),
            P("fsdp"),
            P("fsdp"),
        ),
        check_vma=False,
    )
```

```python
import math

import jax
import jax.numpy as jnp
from jax import lax
from jax.experimental import pallas as pl
from jax.experimental.pallas import tpu as pltpu
from jax.sharding import PartitionSpec as P

norm_eps = 1e-05
beta_one = 0.9
beta_two = 0.95
corr_one = 1.0 - math.exp(200.0 * math.log(0.9))
corr_two = 1.0 - math.exp(200.0 * math.log(0.95))
learn_rate = 0.001
adam_eps = 1e-08
weight_decay = 0.1
outer_beta = 0.9
outer_rate = 0.7

MESH = pl.DeviceIdType.MESH
NX, NZL = 4, 3
NY, NZH, NC = 8, 4, 2
NF, NS = NX * NZL, NY * NZH * NC
FEAT, KVW, TOK = 2304, 512, 256
ROWS = FEAT // NF
XROWS = FEAT // NX
XHALF = XROWS // 2
THALF = TOK // 2
FROWS = 3072
CROWS = FROWS // NC
YROWS = CROWS // NY
YHALF = YROWS // 2
F32, BF16 = jnp.float32, jnp.bfloat16


class Slots:
    def __init__(self):
        self.index = {}

    def __call__(self, *name):
        return self.index.setdefault(name, len(self.index))


def kernel(slots, act_hbm, cot_hbm, w_hbm, gain_hbm, pg_hbm, keys_out, wgrad_out, ggrad_out, delta_out,
           act, w, gain, pg, xhat, xt, xin, relay, cot, wx, kpart, kin1, kin2, kown, zsend, zrecv,
           psend, precv, hsum, ya, yb, yc, yd, zall, dbuf, keys_ref, wgrad_ref, ggrad_ref, lsem, ssem, rsem):
    s, f = lax.axis_index("silo"), lax.axis_index("fsdp")
    core = lax.rem(s, NC)
    zh = lax.rem(s // NC, NZH)
    y = s // (NC * NZH)
    x, zl = f // NZL, lax.rem(f, NZL)

    def silo_at(yy, zz, cc):
        return (yy * NZH + zz) * NC + cc

    def fsdp_at(xx, zz):
        return xx * NZL + zz

    def to_y(d):
        return {"silo": silo_at(lax.rem(y + d, NY), zh, core), "fsdp": f}

    def to_zh(d):
        return {"silo": silo_at(y, lax.rem(zh + d, NZH), core), "fsdp": f}

    def to_zl(d):
        return {"silo": s, "fsdp": fsdp_at(x, lax.rem(zl + d, NZL))}

    def to_x(d):
        return {"silo": s, "fsdp": fsdp_at(lax.rem(x + d + NX, NX), zl)}

    partner = {"silo": silo_at(y, zh, 1 - core), "fsdp": f}
    peers = ([to_y(d) for d in (1, 2, 6, 7)] + [to_zh(d) for d in range(1, NZH)]
             + [to_zl(d) for d in range(1, NZL)] + [to_x(1), to_x(-1)] + [partner])
    pending = []
    results = []

    def result(src, dst):
        copy = pltpu.make_async_copy(src, dst, lsem.at[len(loads) + len(results)])
        copy.start()
        results.append(copy)

    def remote(src, dst, device, *name):
        k = slots(*name)
        return pltpu.make_async_remote_copy(
            src_ref=src, dst_ref=dst, send_sem=ssem.at[k], recv_sem=rsem.at[k],
            device_id=device, device_id_type=MESH)

    def send(src, dst, device, *name):
        copy = remote(src, dst, device, *name)
        copy.start()
        pending.append(copy)

    def arrived(ref, *name):
        remote(ref, ref, partner, *name).wait_recv()

    barrier = pltpu.get_barrier_semaphore()
    for peer in peers:
        pl.semaphore_signal(barrier, inc=1, device_id=peer, device_id_type=MESH)

    loads = [pltpu.make_async_copy(a, b, lsem.at[i]) for i, (a, b) in enumerate((
        (pg_hbm, pg), (cot_hbm.at[0], cot.at[0]), (w_hbm.at[0], w), (gain_hbm, gain), (act_hbm.at[0], act)))]
    for k in (1, 0, 2, 3, 4):
        loads[k].start()

    def rows(start, size):
        return pl.ds(pl.multiple_of(start, 16), size)

    def lanes(start):
        return pg[0, pl.ds(pl.multiple_of(start, 2048), 2048)].reshape(16, 128)

    loads[1].wait()
    pl.semaphore_wait(barrier, len(peers))
    send(cot.at[0], cot.at[1], to_x(1), "c", 1)
    send(cot.at[0], cot.at[3], to_x(-1), "c", -1)

    loads[0].wait()

    def pack_step(i, carry):
        psend[rows(i * 16, 16), :] = lanes((1 - core) * (CROWS * 128) + i * 2048)
        return carry

    lax.fori_loop(0, CROWS // 16, pack_step, 0, unroll=4)

    def at_y(ref, d, start=0, size=YROWS):
        return ref.at[rows(lax.rem(y + d, NY) * YROWS + start, size), :]

    order = (3, 5, 4, 1, 7, 2, 6, 0)
    for d in order:
        send(at_y(psend, d), at_y(precv, d), partner, "pair", d)

    loads[2].wait()
    loads[3].wait()
    diag = lax.broadcasted_iota(jnp.int32, (ROWS, ROWS), 0) == lax.broadcasted_iota(jnp.int32, (ROWS, ROWS), 1)
    gain_row = gain[...].astype(BF16).astype(F32)
    gain_col = jnp.sum(jnp.where(diag, gain_row, 0.0), axis=1, keepdims=True)

    def wrows(zz):
        return wx.at[rows(zz * ROWS, ROWS), :]

    wrows(zl)[...] = (w[...].astype(F32) * gain_col).astype(BF16)
    for d in range(1, NZL):
        send(wrows(zl), wrows(zl), to_zl(d), "wz", d)

    loads[4].wait()

    def norm_step(i, carry):
        at = rows(i * 16, 16)
        wide = act[at, :].astype(F32)
        inv = lax.rsqrt(jnp.sum(wide * wide, axis=1, keepdims=True) * (1.0 / FEAT) + norm_eps)
        xhat[at, :] = (wide * inv).astype(BF16)
        return carry

    lax.fori_loop(0, TOK // 16, norm_step, 0)

    for d in order:
        arrived(at_y(precv, d), "pair", d)
        base = lax.rem(y + d, NY) * YROWS

        def sum_step(i, carry, base=base):
            at = rows(base + i * 16, 16)
            own = lanes(core * (CROWS * 128) + (base + i * 16) * 128)
            hsum[at, :] = (own.astype(F32) + precv[at, :].astype(F32)).astype(BF16)
            return carry

        lax.fori_loop(0, YROWS // 16, sum_step, 0, unroll=4)
        if d == 3:
            send(at_y(hsum, 3), ya.at[0], to_y(1), "ya", 1)
        if d == 5:
            send(at_y(hsum, 5), ya.at[1], to_y(7), "ya", -1)
        if d == 4:
            send(at_y(hsum, 4, 0, YHALF), yb.at[0], to_y(2), "yb", 1)
            send(at_y(hsum, 4, YHALF, YHALF), yb.at[1], to_y(6), "yb", -1)
        if d == 1:
            send(at_y(hsum, 1), yc.at[0], to_y(1), "yc", 1)
        if d == 7:
            send(at_y(hsum, 7), yc.at[1], to_y(7), "yc", -1)

    for j in range(FEAT // 256):
        xt[j * 256:(j + 1) * 256, :] = xhat[:, j * 256:(j + 1) * 256].T

    right, left, far = lax.rem(x + 1, NX), lax.rem(x + 3, NX), lax.rem(x + 2, NX)

    def block(xx):
        return xt.at[rows(xx * XROWS, XROWS), :]

    def half(xx, h):
        return xt.at[rows(xx * XROWS + h * XHALF, XHALF), :]

    send(half(far, 0), relay.at[0], to_x(1), "r", 1)
    send(half(far, 1), relay.at[1], to_x(-1), "r", -1)
    send(block(right), xin.at[0], to_x(1), "x", 1)
    send(block(left), xin.at[2], to_x(-1), "x", -1)

    def combine(d, h, k, sign):
        arrived(ya.at[k], "ya", sign)
        arrived(yb.at[k], "yb", sign)
        near, other = at_y(hsum, d, h * YHALF, YHALF), at_y(hsum, d, (1 - h) * YHALF, YHALF)
        near[...] = (near[...].astype(F32) + ya[k, h * YHALF:(h + 1) * YHALF].astype(F32)
                     + yb[k].astype(F32)).astype(BF16)
        other[...] = (other[...].astype(F32)
                      + ya[k, (1 - h) * YHALF:(2 - h) * YHALF].astype(F32)).astype(BF16)
        send(at_y(hsum, d), yd.at[k], to_y(d), "yd", sign)

    combine(2, 0, 0, 1)
    combine(6, 1, 1, -1)

    arrived(relay.at[0], "r", 1)
    send(relay.at[0], xin.at[1, pl.ds(0, XHALF), :], to_x(1), "f", 1)
    arrived(relay.at[1], "r", -1)
    send(relay.at[1], xin.at[1, pl.ds(XHALF, XHALF), :], to_x(-1), "f", -1)
    arrived(cot.at[1], "c", 1)
    send(cot.at[1, pl.ds(0, THALF), :], cot.at[2, pl.ds(0, THALF), :], to_x(1), "d", 1)
    arrived(cot.at[3], "c", -1)
    send(cot.at[3, pl.ds(THALF, THALF), :], cot.at[2, pl.ds(THALF, THALF), :], to_x(-1), "d", -1)

    total = at_y(hsum, 0)[...].astype(F32)
    for k, sign in ((0, 1), (1, -1)):
        arrived(yc.at[k], "yc", sign)
        total = total + yc[k].astype(F32)
    for k, sign in ((0, 1), (1, -1)):
        arrived(yd.at[k], "yd", sign)
        total = total + yd[k].astype(F32)
    zall[zh] = total.astype(BF16)
    for d in range(1, NZH):
        send(zall.at[zh], zall.at[zh], to_zh(d), "z", d)

    for d in range(1, NZL):
        arrived(wrows(lax.rem(zl - d + NZL, NZL)), "wz", d)

    def partial_keys(ref):
        return lax.dot_general(ref[...], wx[...], (((0,), (0,)), ((), ())), preferred_element_type=F32)

    kown[...] = partial_keys(block(x))
    arrived(xin.at[0], "x", 1)
    kpart[0] = partial_keys(xin.at[0]).astype(BF16)
    arrived(xin.at[2], "x", -1)
    kpart[2] = partial_keys(xin.at[2]).astype(BF16)

    arrived(xin.at[1, pl.ds(0, XHALF), :], "f", 1)
    arrived(xin.at[1, pl.ds(XHALF, XHALF), :], "f", -1)
    kpart[1] = partial_keys(xin.at[1]).astype(BF16)
    send(kpart.at[1, pl.ds(0, THALF), :], kin1.at[0], to_x(1), "k1", 1)
    send(kpart.at[1, pl.ds(THALF, THALF), :], kin1.at[1], to_x(-1), "k1", -1)

    def chunk(d, cc, start=0, size=YROWS):
        return dbuf.at[rows(cc * CROWS + lax.rem(y + d, NY) * YROWS + start, size), :]

    for d in range(1, NZH):
        arrived(zall.at[lax.rem(zh - d + NZH, NZH)], "z", d)
    total = zall[0].astype(F32)
    for k in range(1, NZH):
        total = total + zall[k].astype(F32)
    def deliver(d, cc):
        at = rows(cc * CROWS + lax.rem(y + d, NY) * YROWS, YROWS)
        result(dbuf.at[at, :], delta_out.at[at, :])

    own = chunk(0, core)
    own[...] = (total * (1.0 / NS)).astype(BF16)
    for d in (2, 6, 1, 7):
        send(own, own, to_y(d), "yg", d)
    send(own, own, partner, "cg", 0)
    deliver(0, core)

    arrived(cot.at[2, pl.ds(0, THALF), :], "d", 1)
    arrived(cot.at[2, pl.ds(THALF, THALF), :], "d", -1)

    def product(zz):
        at = rows(zz * ROWS, ROWS)
        out = jnp.dot(xt[rows(x * XROWS + zz * ROWS, ROWS), :], cot[0], preferred_element_type=F32)
        for d in range(1, NX):
            out = out + jnp.dot(xin[d - 1, at, :], cot[d], preferred_element_type=F32)
        return out

    for d in range(1, NZL):
        zsend[d - 1] = product(lax.rem(zl + d, NZL)).astype(BF16)
        send(zsend.at[d - 1], zrecv.at[d - 1], to_zl(d), "gz", d)

    arrived(kin1.at[0], "k1", 1)
    kpart[2, :THALF] = (kpart[2, :THALF].astype(F32) + kin1[0].astype(F32)).astype(BF16)
    send(kpart.at[2], kin2.at[0], to_x(1), "k2", 1)
    arrived(kin1.at[1], "k1", -1)
    kpart[0, THALF:] = (kpart[0, THALF:].astype(F32) + kin1[1].astype(F32)).astype(BF16)
    send(kpart.at[0], kin2.at[1], to_x(-1), "k2", -1)

    wgrad_ref[...] = product(zl)

    arrived(chunk(6, core), "yg", 2)
    send(chunk(6, core), chunk(6, core), to_y(1), "yh", 1)
    send(chunk(6, core, 0, YHALF), chunk(6, core, 0, YHALF), to_y(2), "yi", 1)
    arrived(chunk(2, core), "yg", 6)
    send(chunk(2, core), chunk(2, core), to_y(7), "yh", -1)
    send(chunk(2, core, YHALF, YHALF), chunk(2, core, YHALF, YHALF), to_y(6), "yi", -1)
    send(chunk(6, core), chunk(6, core), partner, "cg", 6)
    deliver(6, core)
    send(chunk(2, core), chunk(2, core), partner, "cg", 2)
    deliver(2, core)
    arrived(chunk(7, core), "yg", 1)
    send(chunk(7, core), chunk(7, core), partner, "cg", 7)
    deliver(7, core)
    arrived(chunk(1, core), "yg", 7)
    send(chunk(1, core), chunk(1, core), partner, "cg", 1)
    deliver(1, core)
    arrived(chunk(5, core), "yh", 1)
    send(chunk(5, core), chunk(5, core), partner, "cg", 5)
    deliver(5, core)
    arrived(chunk(3, core), "yh", -1)
    send(chunk(3, core), chunk(3, core), partner, "cg", 3)
    deliver(3, core)
    arrived(chunk(4, core, 0, YHALF), "yi", 1)
    arrived(chunk(4, core, YHALF, YHALF), "yi", -1)
    send(chunk(4, core), chunk(4, core), partner, "cg", 4)
    deliver(4, core)

    arrived(kin2.at[0], "k2", 1)
    arrived(kin2.at[1], "k2", -1)
    keys_ref[...] = (kown[...] + kin2[0].astype(F32) + kin2[1].astype(F32)).astype(BF16)
    result(keys_ref, keys_out)

    for d in range(1, NZL):
        arrived(zrecv.at[d - 1], "gz", d)
    gsum = wgrad_ref[...] + zrecv[0].astype(F32) + zrecv[1].astype(F32)
    gain_grad = jnp.sum(gsum * w[...].astype(F32), axis=1, keepdims=True)
    wgrad_ref[...] = gsum * gain_col
    ggrad_ref[...] = jnp.sum(jnp.where(diag, gain_grad, 0.0), axis=0, keepdims=True)

    result(wgrad_ref, wgrad_out)
    result(ggrad_ref, ggrad_out)

    for d in (0, 6, 2, 7, 1, 5, 3, 4):
        arrived(chunk(d, 1 - core), "cg", d)
        deliver(d, 1 - core)
    for copy in pending:
        copy.wait_send()
    for copy in results:
        copy.wait()


def exchange(activations, key_cot, key_weight, norm_gain, pseudo_grad):
    slots = Slots()
    count = 64

    def body(*refs):
        kernel(slots, *refs)
        assert len(slots.index) <= count

    hbm = pl.BlockSpec(memory_space=pl.ANY)
    return pl.pallas_call(
        body,
        out_shape=(
            jax.ShapeDtypeStruct((TOK, KVW), BF16),
            jax.ShapeDtypeStruct((ROWS, KVW), F32),
            jax.ShapeDtypeStruct((1, ROWS), F32),
            jax.ShapeDtypeStruct((FROWS, 128), BF16),
        ),
        in_specs=[hbm] * 5,
        out_specs=(hbm,) * 4,
        scratch_shapes=[
            pltpu.VMEM((TOK, FEAT), BF16),
            pltpu.VMEM((ROWS, KVW), BF16),
            pltpu.VMEM((1, ROWS), F32),
            pltpu.VMEM((1, FROWS * 128), BF16),
            pltpu.VMEM((TOK, FEAT), BF16),
            pltpu.VMEM((FEAT, TOK), BF16),
            pltpu.VMEM((NX - 1, XROWS, TOK), BF16),
            pltpu.VMEM((2, XHALF, TOK), BF16),
            pltpu.VMEM((NX, TOK, KVW), BF16),
            pltpu.VMEM((XROWS, KVW), BF16),
            pltpu.VMEM((NX - 1, TOK, KVW), BF16),
            pltpu.VMEM((2, THALF, KVW), BF16),
            pltpu.VMEM((2, TOK, KVW), BF16),
            pltpu.VMEM((TOK, KVW), F32),
            pltpu.VMEM((NZL - 1, ROWS, KVW), BF16),
            pltpu.VMEM((NZL - 1, ROWS, KVW), BF16),
            pltpu.VMEM((CROWS, 128), BF16),
            pltpu.VMEM((CROWS, 128), BF16),
            pltpu.VMEM((CROWS, 128), BF16),
            pltpu.VMEM((2, YROWS, 128), BF16),
            pltpu.VMEM((2, YHALF, 128), BF16),
            pltpu.VMEM((2, YROWS, 128), BF16),
            pltpu.VMEM((2, YROWS, 128), BF16),
            pltpu.VMEM((NZH, YROWS, 128), BF16),
            pltpu.VMEM((FROWS, 128), BF16),
            pltpu.VMEM((TOK, KVW), BF16),
            pltpu.VMEM((ROWS, KVW), F32),
            pltpu.VMEM((1, ROWS), F32),
            pltpu.SemaphoreType.DMA((5 + 3 + 2 * NY,)),
            pltpu.SemaphoreType.DMA((count,)),
            pltpu.SemaphoreType.DMA((count,)),
        ],
        compiler_params=pltpu.CompilerParams(
            collective_id=0, has_side_effects=True, vmem_limit_bytes=56 << 20
        ),
    )(activations, key_cot, key_weight, norm_gain, pseudo_grad)


def adam_step(params, gradient, first_moment, second_moment):
    first_new = beta_one * first_moment + (1.0 - beta_one) * gradient
    second_new = beta_two * second_moment + (1.0 - beta_two) * gradient * gradient
    update = (
        first_new / corr_one / (jnp.sqrt(second_new / corr_two) + adam_eps) + weight_decay * params
    )
    return (params - learn_rate * update, first_new, second_new)


PARTS = 4


def update_kernel(*refs):
    ins, outs, (stage_in, stage_out, sems) = refs[:12], refs[12:21], refs[21:]
    keys, wgrad, ggrad, delta, weight, first, second, gain, gain_first, gain_second, params, mom = stage_in
    started = []

    def copy(src, dst):
        c = pltpu.make_async_copy(src, dst, sems.at[len(started)])
        c.start()
        started.append(c)
        return c

    part = FROWS // PARTS
    pieces = [slice(k * part, (k + 1) * part) for k in range(PARTS)]
    outer_in = []
    for at in pieces:
        outer_in.append([copy(ins[k].at[at, :], stage_in[k].at[at, :]) for k in (3, 10, 11)])
    adam_in = [copy(ins[k], stage_in[k]) for k in (1, 4, 5, 6)]
    gain_in = [copy(ins[k], stage_in[k]) for k in (2, 7, 8, 9)]
    keys_in = copy(ins[0], keys)
    done = []
    for at, waits in zip(pieces, outer_in):
        for c in waits:
            c.wait()
        wide = delta[at, :].astype(F32)
        new_mom = outer_beta * mom[at, :] + wide
        stage_out[7][at, :] = new_mom
        stage_out[6][at, :] = params[at, :] - outer_rate * (wide + outer_beta * new_mom)
        done.append(copy(stage_out[6].at[at, :], outs[7].at[at, :]))
        done.append(copy(stage_out[7].at[at, :], outs[8].at[at, :]))
    keys_in.wait()
    done.append(copy(keys, outs[0]))
    for c in adam_in:
        c.wait()
    new_weight, new_first, new_second = adam_step(
        weight[0].astype(F32), wgrad[...], first[0], second[0]
    )
    stage_out[0][0] = new_weight.astype(BF16)
    stage_out[1][0] = new_first
    stage_out[2][0] = new_second
    for k in range(3):
        done.append(copy(stage_out[k], outs[1 + k]))
    for c in gain_in:
        c.wait()
    for k, value in enumerate(adam_step(gain[...], ggrad[...], gain_first[...], gain_second[...])):
        stage_out[3 + k][...] = value
        done.append(copy(stage_out[3 + k], outs[4 + k]))
    for c in done:
        c.wait()


def update(*arrays):
    hbm = pl.BlockSpec(memory_space=pl.ANY)
    weights, gains, outer = (1, ROWS, KVW), (1, ROWS), (FROWS, 128)
    kinds = (
        ((TOK, KVW), BF16), (weights, BF16), (weights, F32), (weights, F32),
        (gains, F32), (gains, F32), (gains, F32), (outer, F32), (outer, F32),
    )
    return pl.pallas_call(
        update_kernel,
        out_shape=tuple(jax.ShapeDtypeStruct(*kind) for kind in kinds),
        in_specs=[hbm] * 12,
        out_specs=(hbm,) * 9,
        scratch_shapes=[
            tuple(pltpu.VMEM(a.shape, a.dtype) for a in arrays),
            tuple(pltpu.VMEM(*kind) for kind in kinds[1:]),
            pltpu.SemaphoreType.DMA((3 * PARTS + 9 + 2 * PARTS + 7,)),
        ],
        compiler_params=pltpu.CompilerParams(vmem_limit_bytes=56 << 20),
    )(*arrays)


def per_device(
    activations,
    key_cot,
    key_weight,
    weight_first,
    weight_second,
    norm_gain,
    gain_first,
    gain_second,
    pseudo_grad,
    outer_params,
    outer_mom,
):
    keys, weight_grad, gain_grad, delta = exchange(
        activations, key_cot, key_weight, norm_gain, pseudo_grad
    )
    (keys, new_weight, new_first, new_second, new_gain, new_gain_first, new_gain_second, new_params,
     new_mom) = update(
        keys, weight_grad, gain_grad, delta, key_weight, weight_first, weight_second, norm_gain,
        gain_first, gain_second, outer_params.reshape(FROWS, 128), outer_mom.reshape(FROWS, 128),
    )
    return (
        keys[None],
        new_weight,
        new_first,
        new_second,
        new_gain,
        new_gain_first,
        new_gain_second,
        new_params.reshape(-1),
        new_mom.reshape(-1),
    )


def solution(mesh):
    return jax.shard_map(
        per_device,
        mesh=mesh,
        in_specs=(
            P("silo", "fsdp", None),
            P("silo", "fsdp", None),
            P("silo", "fsdp", None),
            P("silo", "fsdp", None),
            P("silo", "fsdp", None),
            P("silo", "fsdp"),
            P("silo", "fsdp"),
            P("silo", "fsdp"),
            P("silo", "fsdp"),
            P("fsdp"),
            P("fsdp"),
        ),
        out_specs=(
            P("silo", "fsdp", None),
            P("silo", "fsdp", None),
            P("silo", "fsdp", None),
            P("silo", "fsdp", None),
            P("silo", "fsdp"),
            P("silo", "fsdp"),
            P("silo", "fsdp"),
            P("fsdp"),
            P("fsdp"),
        ),
        check_vma=False,
    )
```
